128 devices in a mesh: group: 8 (over x, core), slab: 16 (over z, y).
Axes of the slice: x: 4, y: 4, z: 4, core: 2. Of those that a mesh axis runs over, the one named last changes fastest.
Arguments:
- initial_samples: float32 [96, 128, 4096], P('group', 'slab'), may hold values from -6 to 6
- transport_ratios: float32 [3, 128, 4096], P(None, 'slab'), may hold values from 0.05 to 0.33
- assignment: int32 [96], replicated, may hold values from 0 to 95, each once
- obs_values: float32 [512, 512], P(('group', 'slab')), may hold values from -6 to 6
- obs_error: float32 [512, 512], P(('group', 'slab')), may hold values from 0.25 to 4
- sensor_easting_offset: int32 [512, 512], P(('group', 'slab')), may hold values from 0 to 127
- obs_column: int32 [512, 512], P(('group', 'slab')), may hold values from 0 to 23
- obs_count: int32 [512], P(('group', 'slab')), may hold values from 1 to 512, 131072 in all
Outputs:
- analysis: float32 [96, 128, 4096], P('group', 'slab')
The draws below stay inside these ranges and needn't reach their ends.
Inputs may be any that keep to these rules, and one draw needn't show every extreme that they name: `assignment`: a permutation of the members. A block's live observations are its first obs_count entries; some block has exactly 512.
All inputs are finite; a program needn't handle non-finite values.
Results may differ from the reference program's by a relative error of at most 0.0003.
Values sent between devices are 32-bit elements; how exact they have to be, the bound alone decides.
A program may use at most 64 MiB of HBM per device.

```python
import math
import jax
import jax.numpy as jnp
import numpy as np
from jax import lax

MEMBERS = 96
NZ = 64
STEPS = 6
TILE_WIDTH = 8
HC = 8
OBS = 512
ITERS = 8
NX = 128
NYZ = 4096
NB = 512


def touch_ends(entries, key, low, high):
    extent = entries.shape
    index_at = [jax.random.randint(jax.random.fold_in(key, axis), (), 0, extent[axis]) for axis in range(len(extent))]
    entries = entries.at[tuple(index_at)].set(low)
    longest = extent.index(max(extent))
    index_at[longest] = (index_at[longest] + 1) % extent[longest]
    return entries.at[tuple(index_at)].set(high)


def block_levels(stream_key, shape, split, smallest, high):
    factor_of = 1.0
    for axis_at, shards_of in split:
        draws = jax.random.uniform(jax.random.fold_in(jax.random.fold_in(stream_key, 6), axis_at), (shards_of,), jnp.float32, smallest / len(split), high / len(split))
        factor_of = factor_of * jnp.repeat(jnp.exp(draws), shape[axis_at] // shards_of).reshape((-1,) + (1,) * (len(shape) - 1 - axis_at))
    return factor_of


def length_profile(count, total, bound, lean):
    loads = [(1 << 20) // math.isqrt(grade ** lean) + 1 for grade in range(2, count + 1)]
    spare, holding = total - bound - (count - 1), [1] * (count - 1)
    while spare > 0:
        candidates = [i for i in range(count - 1) if holding[i] < bound]
        mass, budget = sum([loads[i] for i in candidates]), spare
        for i in candidates:
            addition = min(bound - holding[i], max(1, budget * loads[i] // mass), spare)
            holding[i] = holding[i] + addition
            spare = spare - addition
    return np.array([bound] + holding)


def uneven(own_key, number_of, total, reach, slope):
    if number_of == 2:
        one = jax.random.randint(own_key, (), max(1, total - reach), min(reach, total - 1) + 1)
        return jnp.stack([one, total - one])
    tallies = jnp.asarray(length_profile(number_of, total, reach, slope), jnp.int32)
    pairs = (number_of - 1) // 2
    giver, receiver = tallies[1:1 + 2 * pairs:2], tallies[2:2 + 2 * pairs:2]
    slack = jnp.minimum(giver - 1, reach - receiver)
    passed = jax.random.randint(jax.random.fold_in(own_key, 1), (pairs,), 0, 1 << 20) % (slack + 1)
    tallies = tallies.at[1:1 + 2 * pairs:2].set(giver - passed).at[2:2 + 2 * pairs:2].set(receiver + passed)
    return tallies[jax.random.permutation(jax.random.fold_in(own_key, 2), number_of)]


def centred(key, extent, scale, reach, split=(), held_as=jnp.bfloat16):
    loudness = block_levels(key, extent, split, -0.22, 0.18) if split else 1.0
    array = jax.random.normal(key, extent, jnp.float32) * scale * loudness
    return jnp.minimum(jnp.maximum(array, -reach), reach).astype(held_as)


def setup_inputs(seed: int = 0) -> dict:
    streams_of = jax.random.split(jax.random.key(seed), 9)
    return {
        "initial_samples": centred(streams_of[0], (MEMBERS, NX, NYZ), 1.0, 6.0, ((0, 8), (1, 16)), jnp.float32),
        "transport_ratios": jnp.clip(0.05 + 0.28 * jax.random.uniform(streams_of[1], (3, NX, NYZ), jnp.float32) ** block_levels(streams_of[1], (3, NX, NYZ), ((1, 16),), -0.2, 0.2), 0.05, 0.33),
        "assignment": jax.random.permutation(streams_of[2], MEMBERS).astype(jnp.int32),
        "obs_values": centred(streams_of[3], (NB, OBS), 1.0, 6.0, ((0, 128),), jnp.float32),
        "obs_error": jnp.clip(jnp.exp(math.log(4.0) - 2.7725887 * jax.random.uniform(streams_of[4], (NB, OBS), jnp.float32) ** block_levels(streams_of[4], (NB, OBS), ((0, 128),), -0.2, 0.2)), 0.25, 4.0),
        "sensor_easting_offset": touch_ends(jax.random.randint(streams_of[5], (NB, OBS), 0, NX), jax.random.fold_in(streams_of[5], 1), 0, NX - 1).astype(jnp.int32),
        "obs_column": touch_ends(jax.random.randint(streams_of[6], (NB, OBS), 0, TILE_WIDTH + 2 * HC), jax.random.fold_in(streams_of[6], 1), 0, (TILE_WIDTH + 2 * HC) - 1).astype(jnp.int32),
        "obs_count": uneven(streams_of[7], NB, NB * OBS // 2, OBS, 2).astype(jnp.int32),
    }


def advance(sample_state, rates):
    z_position = jnp.arange(sample_state.shape[1]) % NZ
    upwind = jnp.roll(sample_state, 1, axis=0)
    below_y = jnp.roll(sample_state, NZ, axis=1)
    below_z = jnp.where(z_position == 0, jnp.roll(sample_state, 1 - NZ, axis=1), jnp.roll(sample_state, 1, axis=1))
    return sample_state - rates[0] * (sample_state - upwind) - rates[1] * (sample_state - below_y) - rates[2] * (sample_state - below_z)

def transport_sample_downstream(sample_state, transport_ratios):
    for section in range(STEPS):
        sample_state = advance(sample_state, transport_ratios)
    return sample_state

def reference(initial_samples, transport_ratios, assignment, obs_values, obs_error, sensor_easting_offset, obs_column, obs_count):
    hi = lax.Precision.HIGHEST
    prior_sample_set = lax.map(lambda sample_state: transport_sample_downstream(sample_state, transport_ratios), initial_samples)
    identity = jnp.eye(MEMBERS, dtype=jnp.float32)
    one_hot = (assignment[:, None] == jnp.arange(MEMBERS, dtype=jnp.int32)[None, :]).astype(jnp.float32)
    slots = jnp.arange(OBS, dtype=jnp.int32)

    def analyse(update_tile):
        vertical_line_positions = (TILE_WIDTH * update_tile - HC + obs_column[update_tile]) % NYZ
        modelled_readings = prior_sample_set[:, sensor_easting_offset[update_tile], vertical_line_positions]
        pred_mean = lax.optimization_barrier(jnp.mean(modelled_readings, axis=0))
        weight = jnp.where(slots < obs_count[update_tile], 1.0 / jnp.sqrt(obs_error[update_tile] * (MEMBERS - 1.0)), 0.0)
        scaled = (modelled_readings - pred_mean) * weight
        innovation = (obs_values[update_tile] - pred_mean) * weight
        gram = identity + jnp.dot(scaled, scaled.T, precision=hi)
        fro_norm = jnp.sqrt(jnp.sum(gram * gram))
        iterate_a = gram / fro_norm
        iterate_z = identity
        for iteration in range(ITERS):
            middle = 1.5 * identity - 0.5 * jnp.dot(iterate_z, iterate_a, precision=hi)
            iterate_a = jnp.dot(iterate_a, middle, precision=hi)
            iterate_z = jnp.dot(middle, iterate_z, precision=hi)
        transform = iterate_z / jnp.sqrt(fro_norm)
        projected = jnp.dot(scaled, innovation, precision=hi)
        mean_weights = jnp.dot(transform, jnp.dot(transform, projected, precision=hi), precision=hi)
        weights_all = mean_weights[:, None] + transform
        ordered = jnp.dot(weights_all, one_hot, precision=hi)
        mesh_volumes = lax.dynamic_slice_in_dim(prior_sample_set, (TILE_WIDTH * update_tile).astype(jnp.int32), TILE_WIDTH, 2)
        cell_mean = lax.optimization_barrier(jnp.mean(mesh_volumes, axis=0))
        return cell_mean[None] + jnp.einsum('mj,mxc->jxc', ordered, mesh_volumes - cell_mean[None], precision=hi)
    blocks = lax.map(analyse, jnp.arange(NB, dtype=jnp.int32))
    return jnp.transpose(blocks, (1, 2, 0, 3)).reshape(MEMBERS, NX, NYZ)
```

```python
import jax
import jax.numpy as jnp
from jax import lax
from jax.experimental import pallas as pl
from jax.experimental.pallas import tpu as pltpu
from jax.sharding import PartitionSpec as P

MEMBERS = 96
NZ = 64
STEPS = 6
TILE_WIDTH = 8
HC = 8
OBS = 512
ITERS = 8

GROUPS = 8
SLABS = 16
DEVICES = GROUPS * SLABS
PLANES = 8
TILES = 32
LANES = 128
QUADS = 3
OWN = 32
BLOCKS = 4
CELLS = PLANES * OWN
ROWS = 112
MESH = pl.DeviceIdType.MESH


def nt(a, b):
    return lax.dot_general(a, b, (((1,), (1,)), ((), ())), preferred_element_type=jnp.float32)


def nn(a, b):
    return lax.dot_general(a, b, (((1,), (0,)), ((), ())), preferred_element_type=jnp.float32)


def halves(a):
    high = a.astype(jnp.bfloat16)
    return high, (a - high.astype(jnp.float32)).astype(jnp.bfloat16)


def product(a, b):
    m = a.shape[0]
    ah, al = halves(a)
    bh, bl = halves(b)
    both = nn(jnp.concatenate([ah, al], axis=0), jnp.concatenate([bh, bl], axis=1))
    return both[:m, :LANES] + (both[:m, LANES:] + both[m:, :LANES])


def swap_rows(tiles, row):
    axis = tiles[0].ndim - 2
    t0, t1, t2, t3 = tiles
    up = (row & 2) == 0
    b0 = jnp.where(up, t0, pltpu.roll(t2, 2, axis))
    b2 = jnp.where(up, pltpu.roll(t0, 6, axis), t2)
    b1 = jnp.where(up, t1, pltpu.roll(t3, 2, axis))
    b3 = jnp.where(up, pltpu.roll(t1, 6, axis), t3)
    even = (row & 1) == 0
    o0 = jnp.where(even, b0, pltpu.roll(b1, 1, axis))
    o1 = jnp.where(even, pltpu.roll(b0, 7, axis), b1)
    o2 = jnp.where(even, b2, pltpu.roll(b3, 1, axis))
    o3 = jnp.where(even, pltpu.roll(b2, 7, axis), b3)
    return o0, o1, o2, o3


def swap_lanes(tiles, lane):
    axis = tiles[0].ndim - 1
    t0, t1, t2, t3 = tiles
    low = (lane & 64) == 0
    b0 = jnp.where(low, t0, pltpu.roll(t2, 64, axis))
    b2 = jnp.where(low, pltpu.roll(t0, 64, axis), t2)
    b1 = jnp.where(low, t1, pltpu.roll(t3, 64, axis))
    b3 = jnp.where(low, pltpu.roll(t1, 64, axis), t3)
    even = (lane & 32) == 0
    o0 = jnp.where(even, b0, pltpu.roll(b1, 32, axis))
    o1 = jnp.where(even, pltpu.roll(b0, 96, axis), b1)
    o2 = jnp.where(even, b2, pltpu.roll(b3, 32, axis))
    o3 = jnp.where(even, pltpu.roll(b2, 96, axis), b3)
    return o0, o1, o2, o3


def iota(shape, dim):
    return lax.broadcasted_iota(jnp.int32, shape, dim)


def kernel(
    x_ref,
    c_ref,
    asg_ref,
    val_ref,
    err_ref,
    east_ref,
    col_ref,
    cnt_ref,
    o_ref,
    state,
    halo_out,
    halo_in,
    outgoing,
    incoming,
    returned,
    split,
    mean_of,
    maps,
    edge_out,
    edge_in,
    acc,
    part_in,
    select,
    ordered,
    halo_send,
    halo_recv,
    edge_send,
    edge_recv,
    part_send,
    part_recv,
    send_sem,
    recv_sem,
    back_send,
    back_recv,
):
    g = lax.axis_index("group")
    s = lax.axis_index("slab")
    me = g * SLABS + s

    def place(d):
        return (d // SLABS, d % SLABS)

    left = place((me + DEVICES - 1) % DEVICES)
    right = place((me + 1) % DEVICES)

    barrier = pltpu.get_barrier_semaphore()

    def greet(i, carry):
        pl.semaphore_signal(
            barrier, inc=1, device_id=place((me + i) % DEVICES), device_id_type=MESH
        )
        return carry

    lax.fori_loop(1, DEVICES, greet, 0)

    row = iota((4, 8, LANES), 1)
    lane = iota((4, 8, LANES), 2)
    first_row = row == 0
    low_half = lane < 64
    z_first = (lane & (NZ - 1)) == 0

    def advance(u, above, carried, tile):
        turned = pltpu.roll(u, 64, 2)
        below_y = jnp.where(low_half, carried, turned)
        below_z = jnp.where(z_first, pltpu.roll(turned, 1, 2), pltpu.roll(u, 1, 2))
        new = (
            u
            - c_ref[0, tile] * (u - above)
            - c_ref[1, tile] * (u - below_y)
            - c_ref[2, tile] * (u - below_z)
        )
        return new, turned

    def source(quad, level):
        if level == 0:
            return lambda tile: x_ref[pl.ds(4 * quad, 4), tile]
        return lambda tile: state[level % 2, tile]

    def levels_of(quad):
        for level in range(STEPS - 1):
            read = source(quad, level)

            def one(tile, carried, level=level, read=read):
                u = read(tile)
                if level == 0:
                    for i in range(4):
                        halo_out[quad, tile, 6 * i : 6 * i + 1] = u[i, 7:8]
                new, turned = advance(u, pltpu.roll(u, 1, 1), carried, tile)
                if level < STEPS - 2:
                    state[(level + 1) % 2, tile] = new
                for i in range(4):
                    at = 6 * i + level + 1
                    halo_out[quad, tile, at : at + 1] = new[i, 7:8]
                return turned

            lax.fori_loop(0, TILES, one, pltpu.roll(read(TILES - 1), 64, 2), unroll=4)

    next_slab = (g, (s + 1) % SLABS)

    def halo_copy(quad):
        return pltpu.make_async_remote_copy(
            src_ref=halo_out.at[quad],
            dst_ref=halo_in.at[quad],
            send_sem=halo_send.at[quad],
            recv_sem=halo_recv.at[quad],
            device_id=next_slab,
            device_id_type=MESH,
        )

    levels_of(0)
    pl.semaphore_wait(barrier, DEVICES - 1)
    halo_copy(0).start()

    def rest(quad, carry):
        levels_of(quad)
        halo_copy(quad).start()
        return carry

    lax.fori_loop(1, QUADS, rest, 0)

    slots = iota((1, OBS), 1)
    for b in range(BLOCKS):
        live = slots < cnt_ref[b : b + 1, :]
        square = jnp.where(live, 1.0 / (err_ref[b : b + 1, :] * (MEMBERS - 1.0)), 0.0)
        valued = square * val_ref[b : b + 1, :]
        easting = east_ref[b : b + 1, :]
        column = TILE_WIDTH * b - HC + col_ref[b : b + 1, :]
        at_slab = iota((SLABS, OBS), 0) == (easting // PLANES)
        left_side = jnp.concatenate(
            [jnp.where(at_slab, square, 0.0), jnp.where(at_slab, valued, 0.0)], axis=0
        )
        high, low = halves(left_side)
        both = jnp.concatenate([high, low], axis=0)
        cell = iota((CELLS, OBS), 0)
        base = (easting % PLANES) * OWN

        def spread(inside, offset):
            at = jnp.where(inside, base + column + offset, -1)
            hot = jnp.where(cell == at, 1.0, 0.0).astype(jnp.bfloat16)
            got = nt(both, hot)
            return got[: 2 * SLABS] + got[2 * SLABS :]

        maps[b] = spread((column >= 0) & (column < OWN), 0)
        if b == 0:
            edge_out[0] = spread(column < 0, OWN)
        if b == BLOCKS - 1:
            edge_out[1] = spread(column >= OWN, -OWN)

    def edge_copy(side):
        return pltpu.make_async_remote_copy(
            src_ref=edge_out.at[side],
            dst_ref=edge_in.at[side],
            send_sem=edge_send.at[side],
            recv_sem=edge_recv.at[side],
            device_id=(left, right)[side],
            device_id_type=MESH,
        )

    edge_copy(0).start()
    edge_copy(1).start()

    spot = iota((LANES, LANES), 0)
    across = iota((LANES, LANES), 1)

    def member(r):
        return 24 * (r // 24) + 12 * ((r // 4) % 2) + 4 * ((r // 8) % 3) + r % 4

    one = jnp.float32(1.0)
    zero = jnp.float32(0.0)
    hot = jnp.where(asg_ref[...] == across, one, zero).astype(jnp.bfloat16)
    order = jnp.where((member(spot) == across) & (spot < MEMBERS), one, zero).astype(jnp.bfloat16)
    slot_rows = nn(order, hot).astype(jnp.bfloat16)
    select[...] = nt(order, slot_rows).astype(jnp.bfloat16)

    def forecast(quad, carry):
        halo_copy(quad).wait_recv()
        for level in range(STEPS):
            read = source(quad, level)

            def one_tile(tile, carried, level=level, read=read):
                u = read(tile)
                upwind = jnp.stack(
                    [
                        jnp.broadcast_to(
                            halo_in[quad, tile, 6 * i + level : 6 * i + level + 1], (8, LANES)
                        )
                        for i in range(4)
                    ]
                )
                above = jnp.where(first_row, upwind, pltpu.roll(u, 1, 1))
                new, turned = advance(u, above, carried, tile)
                if level < STEPS - 1:
                    state[(level + 1) % 2, tile] = new
                else:
                    flat_row = row[0]
                    flat_lane = lane[0]
                    tiles = swap_rows([new[i] for i in range(4)], flat_row)
                    tiles = swap_lanes(tiles, flat_lane)
                    for q in range(4):
                        outgoing[4 * tile + q, quad] = tiles[q]
                return turned

            lax.fori_loop(0, TILES, one_tile, pltpu.roll(read(TILES - 1), 64, 2), unroll=4)
        return carry

    lax.fori_loop(0, QUADS, forecast, 0)

    def message(buffer, to):
        return buffer.at[to[0] * SLABS + to[1]]

    def each_peer(body):
        def at_slab(i, carry):
            def at_group(j, carry):
                peer_g = (g + j) % GROUPS
                peer_s = (s + i) % SLABS

                @pl.when(i * GROUPS + j > 0)
                def _():
                    body(peer_g, peer_s)

                return carry

            return lax.fori_loop(0, GROUPS, at_group, carry)

        lax.fori_loop(0, SLABS, at_slab, 0)

    def send(peer_g, peer_s):
        pltpu.make_async_remote_copy(
            src_ref=message(outgoing, (peer_g, peer_s)),
            dst_ref=incoming.at[s * GROUPS + g],
            send_sem=send_sem,
            recv_sem=recv_sem.at[s],
            device_id=(peer_g, peer_s),
            device_id_type=MESH,
        ).start()

    each_peer(send)
    incoming[s * GROUPS + g] = outgoing[me]

    edge_copy(0).wait_recv()
    edge_copy(1).wait_recv()
    maps[BLOCKS] = edge_in[1]
    maps[BLOCKS + 1] = edge_in[0]
    acc[...] = jnp.zeros(acc.shape, jnp.float32)

    half_row = iota((12, 8, LANES), 1) < 4
    pad = jnp.zeros((LANES - MEMBERS, CELLS), jnp.bfloat16)

    def gather(i, carry):
        from_slab = (s + SLABS - i) % SLABS

        @pl.when(i == 0)
        def _():
            seven = incoming.at[pl.ds(0, GROUPS - 1)]
            pltpu.make_async_copy(seven, seven, recv_sem.at[from_slab]).wait()

        @pl.when(i > 0)
        def _():
            eight = incoming.at[pl.ds(0, GROUPS)]
            pltpu.make_async_copy(eight, eight, recv_sem.at[from_slab]).wait()

        got = incoming[pl.ds(GROUPS * from_slab, GROUPS)].reshape(4, 2, QUADS, 8, LANES)
        a = got[:, 0].reshape(12, 8, LANES)
        b = got[:, 1].reshape(12, 8, LANES)
        near = jnp.where(half_row, a, pltpu.roll(b, 4, 1)).reshape(MEMBERS, LANES)
        far = jnp.where(half_row, pltpu.roll(a, 4, 1), b).reshape(MEMBERS, LANES)
        field = jnp.concatenate([near, far], axis=1)
        mean = jnp.sum(field, axis=0, keepdims=True) * (1.0 / MEMBERS)
        mean_of[from_slab] = mean
        away = field - mean
        high, low = halves(away)
        right_side = jnp.concatenate([high, pad, low, pad], axis=0)
        split[from_slab] = right_side
        pieces = []
        for b in range(BLOCKS + 2):
            omega = maps[b, pl.ds(from_slab, 1)]
            v = maps[b, pl.ds(SLABS + from_slab, 1)]
            pieces.append(omega * away)
            pieces.append(jnp.broadcast_to(v - mean * omega, (ROWS - MEMBERS, CELLS)))
        lhs_high, lhs_low = halves(jnp.concatenate(pieces, axis=0))
        high_part = nt(lhs_high, right_side)
        low_part = nt(lhs_low, right_side[:LANES])
        total = high_part[:, :LANES] + high_part[:, LANES:] + low_part
        acc[...] += total.reshape(acc.shape)
        return carry

    lax.fori_loop(0, SLABS, gather, 0)

    def part_copy(side):
        return pltpu.make_async_remote_copy(
            src_ref=acc.at[BLOCKS + side],
            dst_ref=part_in.at[side],
            send_sem=part_send.at[side],
            recv_sem=part_recv.at[side],
            device_id=(left, right)[side],
            device_id_type=MESH,
        )

    part_copy(0).start()
    part_copy(1).start()

    identity = jnp.where((spot == across) & (spot < MEMBERS), one, zero)
    empty = jnp.zeros((LANES - MEMBERS, LANES), jnp.float32)
    part_copy(0).wait_recv()
    part_copy(1).wait_recv()
    totals = [acc[b] for b in range(BLOCKS)]
    totals[BLOCKS - 1] = totals[BLOCKS - 1] + part_in[0]
    totals[0] = totals[0] + part_in[1]
    grams = [identity + jnp.concatenate([t[:MEMBERS], empty], axis=0) for t in totals]
    fros = [jnp.sqrt(jnp.sum(t * t, keepdims=True)) for t in grams]
    a_of = [t / f for t, f in zip(grams, fros)]
    middles = [1.5 * identity - 0.5 * a for a in a_of]
    z_of = middles
    a_of = [product(a, r) for a, r in zip(a_of, middles)]
    for iteration in range(1, ITERS):
        middles = [1.5 * identity - 0.5 * product(z, a) for z, a in zip(z_of, a_of)]
        if iteration < ITERS - 1:
            a_of = [product(a, r) for a, r in zip(a_of, middles)]
        z_of = [product(r, z) for r, z in zip(middles, z_of)]
    for b in range(BLOCKS):
        transform = z_of[b] * (1.0 / jnp.sqrt(fros[b]))
        projected = jnp.broadcast_to(totals[b][MEMBERS : MEMBERS + 1], (16, LANES))
        mean_weights = product(product(projected, transform), transform)[:1]
        high, low = halves(transform)
        both = nn(select[...], jnp.concatenate([high, low], axis=1))
        by_member = (both[:MEMBERS, :LANES] + both[:MEMBERS, LANES:]) + mean_weights
        high, low = halves(by_member)
        ordered[0, MEMBERS * b : MEMBERS * (b + 1)] = jnp.concatenate([high, high], axis=1)
        ordered[1, MEMBERS * b : MEMBERS * (b + 1)] = jnp.concatenate([low, low], axis=1)

    all_but_one = outgoing.at[pl.ds(0, DEVICES - 1)]
    pltpu.make_async_copy(all_but_one, all_but_one, send_sem).wait()

    block_of = (iota((MEMBERS, CELLS), 1) % OWN) // TILE_WIDTH

    def give_back(i, carry):
        to_slab = (s + i) % SLABS
        right_side = split[to_slab]
        parts = nn(ordered[0], right_side) + nn(ordered[1], right_side)
        field = parts[:MEMBERS]
        for b in range(1, BLOCKS):
            field = jnp.where(block_of == b, parts[MEMBERS * b : MEMBERS * (b + 1)], field)
        field = field + mean_of[to_slab]
        near = field[:, :LANES].reshape(12, 8, LANES)
        far = field[:, LANES:].reshape(12, 8, LANES)
        even = jnp.where(half_row, near, pltpu.roll(far, 4, 1)).reshape(4, QUADS, 8, LANES)
        odd = jnp.where(half_row, pltpu.roll(near, 4, 1), far).reshape(4, QUADS, 8, LANES)
        for a in range(4):
            incoming[GROUPS * to_slab + 2 * a] = even[a]
            incoming[GROUPS * to_slab + 2 * a + 1] = odd[a]

        def to_group(j, carry):
            peer_g = (g + j) % GROUPS

            @pl.when(i * GROUPS + j > 0)
            def _():
                pltpu.make_async_remote_copy(
                    src_ref=incoming.at[GROUPS * to_slab + peer_g],
                    dst_ref=returned.at[me],
                    send_sem=back_send,
                    recv_sem=back_recv,
                    device_id=(peer_g, to_slab),
                    device_id_type=MESH,
                ).start()

            return carry

        lax.fori_loop(0, GROUPS, to_group, 0)
        return carry

    lax.fori_loop(0, SLABS, give_back, 0)
    returned[me] = incoming[s * GROUPS + g]

    for quad in range(QUADS):
        halo_copy(quad).wait_send()
    for side in range(2):
        edge_copy(side).wait_send()
        part_copy(side).wait_send()
    sent = incoming.at[pl.ds(0, DEVICES - 1)]
    pltpu.make_async_copy(sent, sent, back_send).wait()
    got = returned.at[pl.ds(0, DEVICES - 1)]
    pltpu.make_async_copy(got, got, back_recv).wait()

    def unpack(tile, carry):
        for quad in range(QUADS):
            tiles = swap_lanes([returned[4 * tile + q, quad] for q in range(4)], lane[0])
            tiles = swap_rows(tiles, row[0])
            for i in range(4):
                o_ref[4 * quad + i, tile] = tiles[i]
        return carry

    lax.fori_loop(0, TILES, unpack, 0, unroll=2)


def shards(
    initial_samples,
    transport_ratios,
    assignment,
    obs_values,
    obs_error,
    sensor_easting_offset,
    obs_column,
    obs_count,
):
    members, planes, columns = initial_samples.shape

    def tiled(x):
        return jnp.transpose(x.reshape(-1, planes, TILES, LANES), (0, 2, 1, 3))

    f32 = jnp.float32
    bf16 = jnp.bfloat16
    dma = pltpu.SemaphoreType.DMA
    vmem = pl.BlockSpec(memory_space=pltpu.VMEM)
    slot_member = jnp.pad(assignment, (0, LANES - MEMBERS), constant_values=-1)[:, None]
    out = pl.pallas_call(
        kernel,
        name="analysis",
        out_shape=jax.ShapeDtypeStruct((members, TILES, planes, LANES), f32),
        in_specs=[vmem] * 8,
        out_specs=vmem,
        scratch_shapes=[
            pltpu.VMEM((2, TILES, 4, 8, LANES), f32),
            pltpu.VMEM((QUADS, TILES, 24, LANES), f32),
            pltpu.VMEM((QUADS, TILES, 24, LANES), f32),
            pltpu.VMEM((DEVICES, QUADS, 8, LANES), f32),
            pltpu.VMEM((DEVICES, QUADS, 8, LANES), f32),
            pltpu.VMEM((DEVICES, QUADS, 8, LANES), f32),
            pltpu.VMEM((SLABS, 2 * LANES, CELLS), bf16),
            pltpu.VMEM((SLABS, 1, CELLS), f32),
            pltpu.VMEM((BLOCKS + 2, 2 * SLABS, CELLS), f32),
            pltpu.VMEM((2, 2 * SLABS, CELLS), f32),
            pltpu.VMEM((2, 2 * SLABS, CELLS), f32),
            pltpu.VMEM((BLOCKS + 2, ROWS, LANES), f32),
            pltpu.VMEM((2, ROWS, LANES), f32),
            pltpu.VMEM((LANES, LANES), bf16),
            pltpu.VMEM((2, BLOCKS * MEMBERS, 2 * LANES), bf16),
            dma((QUADS,)),
            dma((QUADS,)),
            dma((2,)),
            dma((2,)),
            dma((2,)),
            dma((2,)),
            dma,
            dma((SLABS,)),
            dma,
            dma,
        ],
        compiler_params=pltpu.CompilerParams(
            collective_id=0, has_side_effects=True, vmem_limit_bytes=48 << 20
        ),
    )(
        tiled(initial_samples),
        tiled(transport_ratios),
        slot_member,
        obs_values,
        obs_error,
        sensor_easting_offset,
        obs_column,
        obs_count[:, None],
    )
    return jnp.transpose(out, (0, 2, 1, 3)).reshape(members, planes, columns)


def solution(mesh):
    placed = (
        P("group", "slab", None),
        P(None, "slab", None),
        P(),
        P(("group", "slab"), None),
        P(("group", "slab"), None),
        P(("group", "slab"), None),
        P(("group", "slab"), None),
        P(("group", "slab")),
    )
    return jax.shard_map(
        shards, mesh=mesh, in_specs=placed, out_specs=P("group", "slab", None), check_vma=False
    )
```

```python
import jax
import jax.numpy as jnp
from jax import lax
from jax.experimental import pallas as pl
from jax.experimental.pallas import tpu as pltpu
from jax.sharding import PartitionSpec as P

MEMBERS = 96
NZ = 64
STEPS = 6
TILE_WIDTH = 8
HC = 8
OBS = 512
ITERS = 8

GROUPS = 8
SLABS = 16
DEVICES = GROUPS * SLABS
PLANES = 8
TILES = 32
LANES = 128
QUADS = 3
OWN = 32
BLOCKS = 4
CELLS = PLANES * OWN
ROWS = 112
LOGICAL = pl.DeviceIdType.LOGICAL


def nt(a, b):
    return lax.dot_general(a, b, (((1,), (1,)), ((), ())), preferred_element_type=jnp.float32)


def nn(a, b):
    return lax.dot_general(a, b, (((1,), (0,)), ((), ())), preferred_element_type=jnp.float32)


def halves(a):
    high = a.astype(jnp.bfloat16)
    return high, (a - high.astype(jnp.float32)).astype(jnp.bfloat16)


def product(a, b):
    m = a.shape[0]
    ah, al = halves(a)
    bh, bl = halves(b)
    both = nn(jnp.concatenate([ah, al], axis=0), jnp.concatenate([bh, bl], axis=1))
    return both[:m, :LANES] + (both[:m, LANES:] + both[m:, :LANES])


def swap_rows(tiles, row):
    axis = tiles[0].ndim - 2
    t0, t1, t2, t3 = tiles
    up = (row & 2) == 0
    b0 = jnp.where(up, t0, pltpu.roll(t2, 2, axis))
    b2 = jnp.where(up, pltpu.roll(t0, 6, axis), t2)
    b1 = jnp.where(up, t1, pltpu.roll(t3, 2, axis))
    b3 = jnp.where(up, pltpu.roll(t1, 6, axis), t3)
    even = (row & 1) == 0
    o0 = jnp.where(even, b0, pltpu.roll(b1, 1, axis))
    o1 = jnp.where(even, pltpu.roll(b0, 7, axis), b1)
    o2 = jnp.where(even, b2, pltpu.roll(b3, 1, axis))
    o3 = jnp.where(even, pltpu.roll(b2, 7, axis), b3)
    return o0, o1, o2, o3


def swap_lanes(tiles, lane):
    axis = tiles[0].ndim - 1
    t0, t1, t2, t3 = tiles
    low = (lane & 64) == 0
    b0 = jnp.where(low, t0, pltpu.roll(t2, 64, axis))
    b2 = jnp.where(low, pltpu.roll(t0, 64, axis), t2)
    b1 = jnp.where(low, t1, pltpu.roll(t3, 64, axis))
    b3 = jnp.where(low, pltpu.roll(t1, 64, axis), t3)
    even = (lane & 32) == 0
    o0 = jnp.where(even, b0, pltpu.roll(b1, 32, axis))
    o1 = jnp.where(even, pltpu.roll(b0, 96, axis), b1)
    o2 = jnp.where(even, b2, pltpu.roll(b3, 32, axis))
    o3 = jnp.where(even, pltpu.roll(b2, 96, axis), b3)
    return o0, o1, o2, o3


def iota(shape, dim):
    return lax.broadcasted_iota(jnp.int32, shape, dim)


def transposed(tiles, row):
    axis = tiles[0].ndim - 2
    tiles = list(tiles)
    for d in (4, 2, 1):
        upper = (row & d) == 0
        for j in range(8):
            if not j & d:
                a, b = tiles[j], tiles[j + d]
                tiles[j] = jnp.where(upper, a, pltpu.roll(b, d, axis))
                tiles[j + d] = jnp.where(upper, pltpu.roll(a, 8 - d, axis), b)
    return tiles


def kernel(
    x_hbm,
    c_hbm,
    asg_hbm,
    val_hbm,
    err_hbm,
    east_hbm,
    col_hbm,
    cnt_hbm,
    o_ref,
    x_ref,
    c_ref,
    asg_ref,
    val_ref,
    err_ref,
    east_ref,
    col_ref,
    cnt_ref,
    rates,
    state,
    outgoing,
    incoming,
    returned,
    split,
    mean_of,
    maps,
    edge_out,
    edge_in,
    acc,
    part_in,
    select,
    ordered,
    x_sem,
    small_sem,
    halo_send,
    halo_recv,
    edge_send,
    edge_recv,
    part_send,
    part_recv,
    send_sem,
    recv_sem,
    back_send,
    back_recv,
):
    g = lax.axis_index("group")
    s = lax.axis_index("slab")
    me = g * SLABS + s
    left = (me + DEVICES - 1) % DEVICES
    right = (me + 1) % DEVICES

    rate_copy = pltpu.make_async_copy(c_hbm, c_ref, small_sem.at[0])
    rate_copy.start()

    def sample_copy(quad):
        four = pl.ds(4 * quad, 4)
        return pltpu.make_async_copy(x_hbm.at[four], x_ref.at[four], x_sem.at[quad])

    for quad in range(QUADS):
        sample_copy(quad).start()
    small_copies = [
        pltpu.make_async_copy(source, target, small_sem.at[1 + i])
        for i, (source, target) in enumerate(
            [
                (asg_hbm, asg_ref),
                (val_hbm, val_ref),
                (err_hbm, err_ref),
                (east_hbm, east_ref),
                (col_hbm, col_ref),
                (cnt_hbm, cnt_ref),
            ]
        )
    ]
    for copy in small_copies:
        copy.start()

    barrier = pltpu.get_barrier_semaphore()

    def greet(i, carry):
        pl.semaphore_signal(
            barrier, inc=1, device_id=(me + i) & (DEVICES - 1), device_id_type=LOGICAL
        )
        return carry

    lax.fori_loop(1, DEVICES, greet, 0, unroll=8)

    row = iota((8, LANES), 0)
    lane = iota((8, LANES), 1)
    upper_half = row < 4
    low_half = lane < 64
    z_first = (lane & (NZ - 1)) == 0

    def lanes_swapped(a, b):
        first = jnp.where(low_half, a, pltpu.roll(b, 64, 1))
        second = jnp.where(low_half, pltpu.roll(a, 64, 1), b)
        return jnp.stack([first, second])

    rate_copy.wait()

    def take_rates(u, carry):
        for i in range(3):
            sides = [
                lanes_swapped(c_ref[i, u + 16 * h], c_ref[i, u + 16 * h + 8]) for h in range(2)
            ]
            for x in range(PLANES):
                rates[i, x, pl.ds(2 * u, 2)] = jnp.where(
                    upper_half, sides[0][:, x : x + 1], sides[1][:, x : x + 1]
                )
        return carry

    lax.fori_loop(0, 8, take_rates, 0)

    def wrap(quad, level, first, end):
        last = state[quad, level, first + 1 : end + 1, 16]
        turned = pltpu.roll(last, 64, 2)
        state[quad, level, first + 1 : end + 1, 0] = jnp.where(
            low_half, pltpu.roll(turned, 4, 1), turned
        )

    def take_samples(quad):
        sample_copy(quad).wait()

        def one(u, carry):
            tiles = []
            for h in range(2):
                for i in range(4):
                    at = 4 * quad + i
                    tiles.append(lanes_swapped(x_ref[at, u + 16 * h], x_ref[at, u + 16 * h + 8]))
            for x, tile in enumerate(transposed(tiles, row)):
                state[quad, 0, x + 1, pl.ds(2 * u + 1, 2)] = tile
            return carry

        lax.fori_loop(0, 8, one, 0)
        wrap(quad, 0, 0, PLANES)

    def stepped(quad, level, first, end, ty):
        u = state[quad, level, first + 1 : end + 1, ty + 1]
        above = state[quad, level, first:end, ty + 1]
        below_y = state[quad, level, first + 1 : end + 1, ty]
        below_z = jnp.where(z_first, pltpu.roll(u, 65, 2), pltpu.roll(u, 1, 2))
        return (
            u
            - rates[0, first:end, ty] * (u - above)
            - rates[1, first:end, ty] * (u - below_y)
            - rates[2, first:end, ty] * (u - below_z)
        )

    def advance(quad, level, first, end):
        def one(ty, carry):
            new = stepped(quad, level, first, end, ty)
            state[quad, level + 1, first + 1 : end + 1, ty + 1] = new
            return carry

        lax.fori_loop(0, 16, one, 0, unroll=2)
        wrap(quad, level + 1, first, end)

    def own_cone(quad):
        take_samples(quad)
        for level in range(STEPS - 1):
            advance(quad, level, level + 3, PLANES)

    next_slab = g * SLABS + (s + 1) % SLABS

    def halo_copy(quad):
        return pltpu.make_async_remote_copy(
            src_ref=state.at[quad, :, PLANES, pl.ds(1, 16)],
            dst_ref=state.at[quad, :, 0, pl.ds(1, 16)],
            send_sem=halo_send.at[quad],
            recv_sem=halo_recv.at[quad],
            device_id=next_slab,
            device_id_type=LOGICAL,
        )

    own_cone(0)
    pl.semaphore_wait(barrier, DEVICES - 1)
    halo_copy(0).start()
    own_cone(1)
    halo_copy(1).start()
    own_cone(2)

    for copy in small_copies:
        copy.wait()

    slots = iota((1, OBS), 1)
    for b in range(BLOCKS):
        live = slots < cnt_ref[:, b : b + 1]
        square = jnp.where(live, 1.0 / (err_ref[b : b + 1, :] * (MEMBERS - 1.0)), 0.0)
        valued = square * val_ref[b : b + 1, :]
        easting = east_ref[b : b + 1, :]
        column = TILE_WIDTH * b - HC + col_ref[b : b + 1, :]
        at_slab = iota((SLABS, OBS), 0) == (easting >> 3)
        left_side = jnp.concatenate(
            [jnp.where(at_slab, square, 0.0), jnp.where(at_slab, valued, 0.0)], axis=0
        )
        high, low = halves(left_side)
        both = jnp.concatenate([high, low], axis=0)
        cell = iota((CELLS, OBS), 0)
        base = (easting & (PLANES - 1)) * OWN

        def spread(inside, offset):
            at = jnp.where(inside, base + column + offset, -1)
            hot = jnp.where(cell == at, 1.0, 0.0).astype(jnp.bfloat16)
            got = nt(both, hot)
            return got[: 2 * SLABS] + got[2 * SLABS :]

        maps[b] = spread((column >= 0) & (column < OWN), 0)
        if b == 0:
            edge_out[0] = spread(column < 0, OWN)
        if b == BLOCKS - 1:
            edge_out[1] = spread(column >= OWN, -OWN)

    def edge_copy(side):
        return pltpu.make_async_remote_copy(
            src_ref=edge_out.at[side],
            dst_ref=edge_in.at[side],
            send_sem=edge_send.at[side],
            recv_sem=edge_recv.at[side],
            device_id=(left, right)[side],
            device_id_type=LOGICAL,
        )

    edge_copy(0).start()
    edge_copy(1).start()

    spot = iota((LANES, LANES), 0)
    across = iota((LANES, LANES), 1)

    def member(r):
        return 24 * (r // 24) + 12 * ((r // 4) % 2) + 4 * ((r // 8) % 3) + r % 4

    one = jnp.float32(1.0)
    zero = jnp.float32(0.0)
    slot_lane = iota((LANES, MEMBERS), 1)
    slot_spot = iota((LANES, MEMBERS), 0)
    hot = jnp.where(asg_ref[...] == slot_spot, one, zero).astype(jnp.bfloat16)
    order = jnp.where((member(spot) == across) & (spot < MEMBERS), one, zero).astype(jnp.bfloat16)
    slot_order = jnp.where((member(slot_spot) == slot_lane) & (slot_spot < MEMBERS), one, zero)
    member_rows = nn(order, hot).astype(jnp.bfloat16)
    select[...] = nt(member_rows, slot_order.astype(jnp.bfloat16)).astype(jnp.bfloat16)

    def forecast(quad):
        halo_copy(quad).wait_recv()
        for level in range(STEPS - 1):
            advance(quad, level, 0, level + 3)

        def pack(ty, carry):
            new = stepped(quad, STEPS - 1, 0, PLANES, ty)
            for h in range(2):
                tiles = []
                for x in range(4):
                    a, b = new[x], new[4 + x]
                    if h == 0:
                        tiles.append(jnp.where(upper_half, a, pltpu.roll(b, 4, 0)))
                    else:
                        tiles.append(jnp.where(upper_half, pltpu.roll(a, 4, 0), b))
                for i, tile in enumerate(swap_lanes(tiles, lane)):
                    outgoing[64 * h + 32 * (i // 2) + 2 * ty + i % 2, quad] = tile
            return carry

        lax.fori_loop(0, 16, pack, 0)

    halo_copy(0).wait_send()
    halo_copy(2).start()
    for quad in range(QUADS):
        forecast(quad)

    def each_peer(body):
        def one(k, carry):
            body((g + (k >> 4)) & (GROUPS - 1), (s + k) & (SLABS - 1))
            return carry

        lax.fori_loop(1, DEVICES, one, 0, unroll=2)

    def send(peer_g, peer_s):
        peer = peer_g * SLABS + peer_s
        pltpu.make_async_remote_copy(
            src_ref=outgoing.at[peer],
            dst_ref=incoming.at[s * GROUPS + g],
            send_sem=send_sem,
            recv_sem=recv_sem.at[s],
            device_id=peer,
            device_id_type=LOGICAL,
        ).start()

    each_peer(send)
    incoming[s * GROUPS + g] = outgoing[me]

    edge_copy(0).wait_recv()
    edge_copy(1).wait_recv()
    maps[BLOCKS] = edge_in[1]
    maps[BLOCKS + 1] = edge_in[0]
    acc[...] = jnp.zeros(acc.shape, jnp.float32)

    half_row = iota((12, 8, LANES), 1) < 4
    pad = jnp.zeros((LANES - MEMBERS, CELLS), jnp.bfloat16)

    def gather(i, carry):
        from_slab = (s + SLABS - i) % SLABS

        @pl.when(i == 0)
        def _():
            seven = incoming.at[pl.ds(0, GROUPS - 1)]
            pltpu.make_async_copy(seven, seven, recv_sem.at[from_slab]).wait()

        @pl.when(i > 0)
        def _():
            eight = incoming.at[pl.ds(0, GROUPS)]
            pltpu.make_async_copy(eight, eight, recv_sem.at[from_slab]).wait()

        got = incoming[pl.ds(GROUPS * from_slab, GROUPS)].reshape(4, 2, QUADS, 8, LANES)
        a = got[:, 0].reshape(12, 8, LANES)
        b = got[:, 1].reshape(12, 8, LANES)
        near = jnp.where(half_row, a, pltpu.roll(b, 4, 1)).reshape(MEMBERS, LANES)
        far = jnp.where(half_row, pltpu.roll(a, 4, 1), b).reshape(MEMBERS, LANES)
        field = jnp.concatenate([near, far], axis=1)
        mean = jnp.sum(field, axis=0, keepdims=True) * (1.0 / MEMBERS)
        mean_of[from_slab] = mean
        away = field - mean
        high, low = halves(away)
        right_side = jnp.concatenate([high, pad, low, pad], axis=0)
        split[from_slab] = right_side
        pieces = []
        for b in range(BLOCKS + 2):
            omega = maps[b, pl.ds(from_slab, 1)]
            v = maps[b, pl.ds(SLABS + from_slab, 1)]
            pieces.append(omega * away)
            pieces.append(jnp.broadcast_to(v - mean * omega, (ROWS - MEMBERS, CELLS)))
        lhs_high, lhs_low = halves(jnp.concatenate(pieces, axis=0))
        high_part = nt(lhs_high, right_side)
        low_part = nt(lhs_low, right_side[:LANES])
        total = high_part[:, :LANES] + high_part[:, LANES:] + low_part
        acc[...] += total.reshape(acc.shape)
        return carry

    lax.fori_loop(0, SLABS, gather, 0)

    def part_copy(side):
        return pltpu.make_async_remote_copy(
            src_ref=acc.at[BLOCKS + side],
            dst_ref=part_in.at[side],
            send_sem=part_send.at[side],
            recv_sem=part_recv.at[side],
            device_id=(left, right)[side],
            device_id_type=LOGICAL,
        )

    part_copy(0).start()
    part_copy(1).start()

    identity = jnp.where((spot == across) & (spot < MEMBERS), one, zero)
    empty = jnp.zeros((LANES - MEMBERS, LANES), jnp.float32)
    part_copy(0).wait_recv()
    part_copy(1).wait_recv()
    totals = [acc[b] for b in range(BLOCKS)]
    totals[BLOCKS - 1] = totals[BLOCKS - 1] + part_in[0]
    totals[0] = totals[0] + part_in[1]
    grams = [identity + jnp.concatenate([t[:MEMBERS], empty], axis=0) for t in totals]
    fros = [jnp.sqrt(jnp.sum(t * t, keepdims=True)) for t in grams]
    a_of = [t / f for t, f in zip(grams, fros)]
    middles = [1.5 * identity - 0.5 * a for a in a_of]
    z_of = middles
    a_of = [product(a, r) for a, r in zip(a_of, middles)]
    for iteration in range(1, ITERS):
        middles = [1.5 * identity - 0.5 * product(z, a) for z, a in zip(z_of, a_of)]
        if iteration < ITERS - 1:
            a_of = [product(a, r) for a, r in zip(a_of, middles)]
        z_of = [product(r, z) for r, z in zip(middles, z_of)]
    for b in range(BLOCKS):
        transform = z_of[b] * (1.0 / jnp.sqrt(fros[b]))
        projected = jnp.broadcast_to(totals[b][MEMBERS : MEMBERS + 1], (16, LANES))
        mean_weights = product(product(projected, transform), transform)[:1]
        high, low = halves(transform)
        both = nn(select[...], jnp.concatenate([high, low], axis=1))
        by_member = (both[:MEMBERS, :LANES] + both[:MEMBERS, LANES:]) + mean_weights
        high, low = halves(by_member)
        ordered[0, MEMBERS * b : MEMBERS * (b + 1)] = jnp.concatenate([high, high], axis=1)
        ordered[1, MEMBERS * b : MEMBERS * (b + 1)] = jnp.concatenate([low, low], axis=1)

    all_but_one = outgoing.at[pl.ds(0, DEVICES - 1)]
    pltpu.make_async_copy(all_but_one, all_but_one, send_sem).wait()

    block_of = (iota((MEMBERS, CELLS), 1) % OWN) // TILE_WIDTH

    def give_back(i, carry):
        to_slab = (s + i) % SLABS
        right_side = split[to_slab]
        parts = nn(ordered[0], right_side) + nn(ordered[1], right_side)
        field = parts[:MEMBERS]
        for b in range(1, BLOCKS):
            field = jnp.where(block_of == b, parts[MEMBERS * b : MEMBERS * (b + 1)], field)
        field = field + mean_of[to_slab]
        near = field[:, :LANES].reshape(12, 8, LANES)
        far = field[:, LANES:].reshape(12, 8, LANES)
        even = jnp.where(half_row, near, pltpu.roll(far, 4, 1)).reshape(4, QUADS, 8, LANES)
        odd = jnp.where(half_row, pltpu.roll(near, 4, 1), far).reshape(4, QUADS, 8, LANES)
        for a in range(4):
            incoming[GROUPS * to_slab + 2 * a] = even[a]
            incoming[GROUPS * to_slab + 2 * a + 1] = odd[a]

        def to_group(j, carry):
            peer_g = (g + j) & (GROUPS - 1)

            @pl.when(i * GROUPS + j > 0)
            def _():
                pltpu.make_async_remote_copy(
                    src_ref=incoming.at[GROUPS * to_slab + peer_g],
                    dst_ref=returned.at[me],
                    send_sem=back_send,
                    recv_sem=back_recv,
                    device_id=peer_g * SLABS + to_slab,
                    device_id_type=LOGICAL,
                ).start()

            return carry

        lax.fori_loop(0, GROUPS, to_group, 0)
        return carry

    lax.fori_loop(0, SLABS, give_back, 0)
    returned[me] = incoming[s * GROUPS + g]

    halo_copy(1).wait_send()
    halo_copy(2).wait_send()
    for side in range(2):
        edge_copy(side).wait_send()
        part_copy(side).wait_send()
    sent = incoming.at[pl.ds(0, DEVICES - 1)]
    pltpu.make_async_copy(sent, sent, back_send).wait()
    got = returned.at[pl.ds(0, DEVICES - 1)]
    pltpu.make_async_copy(got, got, back_recv).wait()

    def unpack(tile, carry):
        for quad in range(QUADS):
            tiles = swap_lanes([returned[4 * tile + q, quad] for q in range(4)], lane)
            tiles = swap_rows(tiles, row)
            for i in range(4):
                o_ref[4 * quad + i, tile] = tiles[i]
        return carry

    lax.fori_loop(0, TILES, unpack, 0, unroll=2)


def shards(
    initial_samples,
    transport_ratios,
    assignment,
    obs_values,
    obs_error,
    sensor_easting_offset,
    obs_column,
    obs_count,
):
    members, planes, columns = initial_samples.shape

    def tiled(x):
        return jnp.transpose(x.reshape(-1, planes, TILES, LANES), (0, 2, 1, 3))

    f32 = jnp.float32
    i32 = jnp.int32
    bf16 = jnp.bfloat16
    dma = pltpu.SemaphoreType.DMA
    hbm = pl.BlockSpec(memory_space=pltpu.HBM)
    out = pl.pallas_call(
        kernel,
        name="analysis",
        out_shape=jax.ShapeDtypeStruct((members, TILES, planes, LANES), f32),
        in_specs=[hbm] * 8,
        out_specs=pl.BlockSpec(memory_space=pltpu.VMEM),
        scratch_shapes=[
            pltpu.VMEM((4 * QUADS, TILES, PLANES, LANES), f32),
            pltpu.VMEM((3, TILES, PLANES, LANES), f32),
            pltpu.VMEM((1, MEMBERS), i32),
            pltpu.VMEM((BLOCKS, OBS), f32),
            pltpu.VMEM((BLOCKS, OBS), f32),
            pltpu.VMEM((BLOCKS, OBS), i32),
            pltpu.VMEM((BLOCKS, OBS), i32),
            pltpu.VMEM((1, BLOCKS), i32),
            pltpu.VMEM((3, PLANES, 16, 8, LANES), f32),
            pltpu.VMEM((QUADS, STEPS, PLANES + 1, 17, 8, LANES), f32),
            pltpu.VMEM((DEVICES, QUADS, 8, LANES), f32),
            pltpu.VMEM((DEVICES, QUADS, 8, LANES), f32),
            pltpu.VMEM((DEVICES, QUADS, 8, LANES), f32),
            pltpu.VMEM((SLABS, 2 * LANES, CELLS), bf16),
            pltpu.VMEM((SLABS, 1, CELLS), f32),
            pltpu.VMEM((BLOCKS + 2, 2 * SLABS, CELLS), f32),
            pltpu.VMEM((2, 2 * SLABS, CELLS), f32),
            pltpu.VMEM((2, 2 * SLABS, CELLS), f32),
            pltpu.VMEM((BLOCKS + 2, ROWS, LANES), f32),
            pltpu.VMEM((2, ROWS, LANES), f32),
            pltpu.VMEM((LANES, LANES), bf16),
            pltpu.VMEM((2, BLOCKS * MEMBERS, 2 * LANES), bf16),
            dma((QUADS,)),
            dma((7,)),
            dma((QUADS,)),
            dma((QUADS,)),
            dma((2,)),
            dma((2,)),
            dma((2,)),
            dma((2,)),
            dma,
            dma((SLABS,)),
            dma,
            dma,
        ],
        compiler_params=pltpu.CompilerParams(
            collective_id=0, has_side_effects=True, vmem_limit_bytes=56 << 20
        ),
    )(
        tiled(initial_samples),
        tiled(transport_ratios),
        assignment[None, :],
        obs_values,
        obs_error,
        sensor_easting_offset,
        obs_column,
        obs_count[None, :],
    )
    return jnp.transpose(out, (0, 2, 1, 3)).reshape(members, planes, columns)


def solution(mesh):
    placed = (
        P("group", "slab", None),
        P(None, "slab", None),
        P(),
        P(("group", "slab"), None),
        P(("group", "slab"), None),
        P(("group", "slab"), None),
        P(("group", "slab"), None),
        P(("group", "slab")),
    )
    return jax.shard_map(
        shards, mesh=mesh, in_specs=placed, out_specs=P("group", "slab", None), check_vma=False
    )
```

```python
import jax
import jax.numpy as jnp
from jax import lax
from jax.experimental import pallas as pl
from jax.experimental.pallas import tpu as pltpu
from jax.sharding import PartitionSpec as P

MEMBERS = 96
NZ = 64
STEPS = 6
TILE_WIDTH = 8
HC = 8
OBS = 512
ITERS = 8

GROUPS = 8
SLABS = 16
DEVICES = GROUPS * SLABS
PLANES = 8
TILES = 32
LANES = 128
QUADS = 3
OWN = 32
BLOCKS = 4
CELLS = PLANES * OWN
ROWS = 112
LOGICAL = pl.DeviceIdType.LOGICAL


def nt(a, b):
    return lax.dot_general(a, b, (((1,), (1,)), ((), ())), preferred_element_type=jnp.float32)


def nn(a, b):
    return lax.dot_general(a, b, (((1,), (0,)), ((), ())), preferred_element_type=jnp.float32)


def halves(a):
    high = a.astype(jnp.bfloat16)
    return high, (a - high.astype(jnp.float32)).astype(jnp.bfloat16)


def product(a, b):
    m = a.shape[0]
    ah, al = halves(a)
    bh, bl = halves(b)
    both = nn(jnp.concatenate([ah, al], axis=0), jnp.concatenate([bh, bl], axis=1))
    return both[:m, :LANES] + (both[:m, LANES:] + both[m:, :LANES])


def swap_rows(tiles, row):
    axis = tiles[0].ndim - 2
    t0, t1, t2, t3 = tiles
    up = (row & 2) == 0
    b0 = jnp.where(up, t0, pltpu.roll(t2, 2, axis))
    b2 = jnp.where(up, pltpu.roll(t0, 6, axis), t2)
    b1 = jnp.where(up, t1, pltpu.roll(t3, 2, axis))
    b3 = jnp.where(up, pltpu.roll(t1, 6, axis), t3)
    even = (row & 1) == 0
    o0 = jnp.where(even, b0, pltpu.roll(b1, 1, axis))
    o1 = jnp.where(even, pltpu.roll(b0, 7, axis), b1)
    o2 = jnp.where(even, b2, pltpu.roll(b3, 1, axis))
    o3 = jnp.where(even, pltpu.roll(b2, 7, axis), b3)
    return o0, o1, o2, o3


def swap_lanes(tiles, lane):
    axis = tiles[0].ndim - 1
    t0, t1, t2, t3 = tiles
    low = (lane & 64) == 0
    b0 = jnp.where(low, t0, pltpu.roll(t2, 64, axis))
    b2 = jnp.where(low, pltpu.roll(t0, 64, axis), t2)
    b1 = jnp.where(low, t1, pltpu.roll(t3, 64, axis))
    b3 = jnp.where(low, pltpu.roll(t1, 64, axis), t3)
    even = (lane & 32) == 0
    o0 = jnp.where(even, b0, pltpu.roll(b1, 32, axis))
    o1 = jnp.where(even, pltpu.roll(b0, 96, axis), b1)
    o2 = jnp.where(even, b2, pltpu.roll(b3, 32, axis))
    o3 = jnp.where(even, pltpu.roll(b2, 96, axis), b3)
    return o0, o1, o2, o3


def iota(shape, dim):
    return lax.broadcasted_iota(jnp.int32, shape, dim)


def transposed(tiles, row):
    axis = tiles[0].ndim - 2
    tiles = list(tiles)
    for d in (4, 2, 1):
        upper = (row & d) == 0
        for j in range(8):
            if not j & d:
                a, b = tiles[j], tiles[j + d]
                tiles[j] = jnp.where(upper, a, pltpu.roll(b, d, axis))
                tiles[j + d] = jnp.where(upper, pltpu.roll(a, 8 - d, axis), b)
    return tiles


def kernel(
    x_hbm,
    c_hbm,
    asg_hbm,
    val_hbm,
    err_hbm,
    east_hbm,
    col_hbm,
    cnt_hbm,
    o_ref,
    x_ref,
    c_ref,
    asg_ref,
    val_ref,
    err_ref,
    east_ref,
    col_ref,
    cnt_ref,
    c_next,
    rates,
    state,
    ahead,
    outgoing,
    incoming,
    returned,
    split,
    mean_of,
    maps,
    edge_out,
    edge_in,
    acc,
    part_in,
    select,
    ordered,
    x_sem,
    small_sem,
    halo_send,
    halo_recv,
    edge_send,
    edge_recv,
    part_send,
    part_recv,
    send_sem,
    recv_sem,
    back_send,
    back_recv,
):
    g = lax.axis_index("group")
    s = lax.axis_index("slab")
    me = g * SLABS + s
    left = (me + DEVICES - 1) % DEVICES
    right = (me + 1) % DEVICES

    rate_copy = pltpu.make_async_copy(c_hbm, c_ref, small_sem.at[0])
    rate_copy.start()

    def sample_copy(quad):
        four = pl.ds(4 * quad, 4)
        return pltpu.make_async_copy(x_hbm.at[four], x_ref.at[four], x_sem.at[quad])

    for quad in range(QUADS):
        sample_copy(quad).start()
    small_copies = [
        pltpu.make_async_copy(source, target, small_sem.at[1 + i])
        for i, (source, target) in enumerate(
            [
                (asg_hbm, asg_ref),
                (val_hbm, val_ref),
                (err_hbm, err_ref),
                (east_hbm, east_ref),
                (col_hbm, col_ref),
                (cnt_hbm, cnt_ref),
            ]
        )
    ]
    for copy in small_copies:
        copy.start()

    barrier = pltpu.get_barrier_semaphore()

    def greet(i, carry):
        pl.semaphore_signal(
            barrier, inc=1, device_id=(me + i) & (DEVICES - 1), device_id_type=LOGICAL
        )
        return carry

    lax.fori_loop(1, DEVICES, greet, 0, unroll=8)

    row = iota((8, LANES), 0)
    lane = iota((8, LANES), 1)
    upper_half = row < 4
    low_half = lane < 64
    z_first = (lane & (NZ - 1)) == 0

    def lanes_swapped(a, b):
        first = jnp.where(low_half, a, pltpu.roll(b, 64, 1))
        second = jnp.where(low_half, pltpu.roll(a, 64, 1), b)
        return jnp.stack([first, second])

    rate_copy.wait()

    def take_rates(source, planes, offset):
        def one(u, carry):
            for i in range(3):
                sides = [
                    lanes_swapped(source[i, u + 16 * h], source[i, u + 16 * h + 8])
                    for h in range(2)
                ]
                for x in range(planes):
                    rates[i, offset + x, pl.ds(2 * u, 2)] = jnp.where(
                        upper_half, sides[0][:, x : x + 1], sides[1][:, x : x + 1]
                    )
            return carry

        lax.fori_loop(0, 8, one, 0)

    take_rates(c_ref, PLANES, 0)

    def wrap(grid, level, first, end):
        last = grid[level, first + 1 : end + 1, 16]
        turned = pltpu.roll(last, 64, 2)
        grid[level, first + 1 : end + 1, 0] = jnp.where(
            low_half, pltpu.roll(turned, 4, 1), turned
        )

    def take_samples(quad, grid):
        sample_copy(quad).wait()

        def one(u, carry):
            tiles = []
            for h in range(2):
                for i in range(4):
                    at = 4 * quad + i
                    tiles.append(lanes_swapped(x_ref[at, u + 16 * h], x_ref[at, u + 16 * h + 8]))
            for x, tile in enumerate(transposed(tiles, row)):
                grid[0, x + 1, pl.ds(2 * u + 1, 2)] = tile
            return carry

        lax.fori_loop(0, 8, one, 0)
        wrap(grid, 0, 0, PLANES)

    def stepped(grid, level, first, end, ty, n):
        u = grid[level, first + 1 : end + 1, pl.ds(ty + 1, n)]
        above = grid[level, first:end, pl.ds(ty + 1, n)]
        below_y = grid[level, first + 1 : end + 1, pl.ds(ty, n)]
        below_z = jnp.where(z_first, pltpu.roll(u, 65, 3), pltpu.roll(u, 1, 3))
        return (
            u
            - rates[0, first:end, pl.ds(ty, n)] * (u - above)
            - rates[1, first:end, pl.ds(ty, n)] * (u - below_y)
            - rates[2, first:end, pl.ds(ty, n)] * (u - below_z)
        )

    def advance(grid, level, first, end):
        planes = end - first
        n = 16 if planes < 3 else 8 if planes < 6 else 4

        def one(i, carry):
            new = stepped(grid, level, first, end, n * i, n)
            grid[level + 1, first + 1 : end + 1, pl.ds(n * i + 1, n)] = new
            return carry

        lax.fori_loop(0, 16 // n, one, 0)
        wrap(grid, level + 1, first, end)

    next_slab = g * SLABS + ((s + 1) & (SLABS - 1))
    last_slab = g * SLABS + ((s + SLABS - 1) & (SLABS - 1))

    def halo_copy(quad):
        return pltpu.make_async_remote_copy(
            src_ref=state.at[quad, :, PLANES, pl.ds(1, 16)],
            dst_ref=state.at[quad, :, 0, pl.ds(1, 16)],
            send_sem=halo_send.at[quad],
            recv_sem=halo_recv.at[quad],
            device_id=next_slab,
            device_id_type=LOGICAL,
        )

    back_halo = pltpu.make_async_remote_copy(
        src_ref=ahead.at[0, pl.ds(1, STEPS), pl.ds(1, 16)],
        dst_ref=ahead.at[0, pl.ds(PLANES + 1, STEPS), pl.ds(1, 16)],
        send_sem=halo_send.at[2],
        recv_sem=halo_recv.at[2],
        device_id=last_slab,
        device_id_type=LOGICAL,
    )
    back_rates = pltpu.make_async_remote_copy(
        src_ref=c_ref,
        dst_ref=c_next,
        send_sem=halo_send.at[3],
        recv_sem=halo_recv.at[3],
        device_id=last_slab,
        device_id_type=LOGICAL,
    )

    grids = [state.at[0], state.at[1]]
    for quad in range(2):
        take_samples(quad, grids[quad])
        for level in range(STEPS - 1):
            advance(grids[quad], level, level + 3, PLANES)
    take_samples(2, ahead)

    pl.semaphore_wait(barrier, DEVICES - 1)
    halo_copy(0).start()
    back_rates.start()
    back_halo.start()
    for level in range(STEPS - 1):
        advance(ahead, level, level + 1, PLANES)

    for copy in small_copies:
        copy.wait()

    slots = iota((1, OBS), 1)
    for b in range(BLOCKS):
        live = slots < cnt_ref[:, b : b + 1]
        square = jnp.where(live, 1.0 / (err_ref[b : b + 1, :] * (MEMBERS - 1.0)), 0.0)
        valued = square * val_ref[b : b + 1, :]
        easting = east_ref[b : b + 1, :]
        column = TILE_WIDTH * b - HC + col_ref[b : b + 1, :]
        at_slab = iota((SLABS, OBS), 0) == (easting >> 3)
        left_side = jnp.concatenate(
            [jnp.where(at_slab, square, 0.0), jnp.where(at_slab, valued, 0.0)], axis=0
        )
        high, low = halves(left_side)
        both = jnp.concatenate([high, low], axis=0)
        cell = iota((CELLS, OBS), 0)
        base = (easting & (PLANES - 1)) * OWN

        def spread(inside, offset):
            at = jnp.where(inside, base + column + offset, -1)
            hot = jnp.where(cell == at, 1.0, 0.0).astype(jnp.bfloat16)
            got = nt(both, hot)
            return got[: 2 * SLABS] + got[2 * SLABS :]

        maps[b] = spread((column >= 0) & (column < OWN), 0)
        if b == 0:
            edge_out[0] = spread(column < 0, OWN)
        if b == BLOCKS - 1:
            edge_out[1] = spread(column >= OWN, -OWN)

    def edge_copy(side):
        return pltpu.make_async_remote_copy(
            src_ref=edge_out.at[side],
            dst_ref=edge_in.at[side],
            send_sem=edge_send.at[side],
            recv_sem=edge_recv.at[side],
            device_id=(left, right)[side],
            device_id_type=LOGICAL,
        )

    edge_copy(0).start()
    edge_copy(1).start()

    spot = iota((LANES, LANES), 0)
    across = iota((LANES, LANES), 1)

    def member(r):
        return 24 * (r // 24) + 12 * ((r // 4) % 2) + 4 * ((r // 8) % 3) + r % 4

    one = jnp.float32(1.0)
    zero = jnp.float32(0.0)
    slot_lane = iota((LANES, MEMBERS), 1)
    slot_spot = iota((LANES, MEMBERS), 0)
    hot = jnp.where(asg_ref[...] == slot_spot, one, zero).astype(jnp.bfloat16)
    order = jnp.where((member(spot) == across) & (spot < MEMBERS), one, zero).astype(jnp.bfloat16)
    slot_order = jnp.where((member(slot_spot) == slot_lane) & (slot_spot < MEMBERS), one, zero)
    member_rows = nn(order, hot).astype(jnp.bfloat16)
    select[...] = nt(member_rows, slot_order.astype(jnp.bfloat16)).astype(jnp.bfloat16)

    def pack_all(quad, grid, first):
        def pack(i, carry):
            ty = 4 * i
            new = stepped(grid, STEPS - 1, first, first + PLANES, ty, 4)
            at_plane = [new[(x - first) % PLANES] for x in range(PLANES)]
            for h in range(2):
                tiles = []
                for x in range(4):
                    a, b = at_plane[x], at_plane[4 + x]
                    if h == 0:
                        tiles.append(jnp.where(upper_half, a, pltpu.roll(b, 4, 1)))
                    else:
                        tiles.append(jnp.where(upper_half, pltpu.roll(a, 4, 1), b))
                for j, tile in enumerate(swap_lanes(tiles, lane)):
                    for k in range(4):
                        at = 64 * h + 32 * (j // 2) + 2 * k + j % 2
                        outgoing[at + 2 * ty, quad] = tile[k]
            return carry

        lax.fori_loop(0, 4, pack, 0)

    def forecast(quad):
        halo_copy(quad).wait_recv()
        for level in range(STEPS - 1):
            advance(grids[quad], level, 0, level + 3)
        pack_all(quad, grids[quad], 0)

    halo_copy(0).wait_send()
    halo_copy(1).start()
    forecast(0)
    back_rates.wait_recv()
    take_rates(c_next, STEPS, PLANES)
    back_halo.wait_recv()
    wrap(ahead, 0, PLANES, PLANES + STEPS)
    for level in range(STEPS - 1):
        advance(ahead, level, PLANES, PLANES + STEPS)
    pack_all(2, ahead, STEPS)
    forecast(1)

    def each_peer(body):
        def one(k, carry):
            body((g + (k >> 4)) & (GROUPS - 1), (s + k) & (SLABS - 1))
            return carry

        lax.fori_loop(1, DEVICES, one, 0, unroll=2)

    def send(peer_g, peer_s):
        peer = peer_g * SLABS + peer_s
        pltpu.make_async_remote_copy(
            src_ref=outgoing.at[peer],
            dst_ref=incoming.at[s * GROUPS + g],
            send_sem=send_sem,
            recv_sem=recv_sem.at[s],
            device_id=peer,
            device_id_type=LOGICAL,
        ).start()

    each_peer(send)
    incoming[s * GROUPS + g] = outgoing[me]

    edge_copy(0).wait_recv()
    edge_copy(1).wait_recv()
    maps[BLOCKS] = edge_in[1]
    maps[BLOCKS + 1] = edge_in[0]
    acc[...] = jnp.zeros(acc.shape, jnp.float32)

    half_row = iota((12, 8, LANES), 1) < 4
    pad = jnp.zeros((LANES - MEMBERS, CELLS), jnp.bfloat16)

    late = (iota((GROUPS, 8, LANES), 1) >= 4) & (iota((GROUPS, 8, LANES), 2) >= 64)
    seven = incoming.at[pl.ds(0, GROUPS - 1)]
    pltpu.make_async_copy(seven, seven, recv_sem.at[s]).wait()

    def gather(i, carry):
        from_slab = (s - i) & (SLABS - 1)
        before = (s - i - 1) & (SLABS - 1)

        @pl.when(i < SLABS - 1)
        def _():
            eight = incoming.at[pl.ds(0, GROUPS)]
            pltpu.make_async_copy(eight, eight, recv_sem.at[before]).wait()

        got = incoming[pl.ds(GROUPS * from_slab, GROUPS)]
        third = jnp.where(late, got[:, 2], incoming[pl.ds(GROUPS * before, GROUPS), 2])
        got = jnp.concatenate([got[:, :2], third[:, None]], axis=1).reshape(4, 2, QUADS, 8, LANES)
        a = got[:, 0].reshape(12, 8, LANES)
        b = got[:, 1].reshape(12, 8, LANES)
        near = jnp.where(half_row, a, pltpu.roll(b, 4, 1)).reshape(MEMBERS, LANES)
        far = jnp.where(half_row, pltpu.roll(a, 4, 1), b).reshape(MEMBERS, LANES)
        field = jnp.concatenate([near, far], axis=1)
        mean = jnp.sum(field, axis=0, keepdims=True) * (1.0 / MEMBERS)
        mean_of[from_slab] = mean
        away = field - mean
        high, low = halves(away)
        right_side = jnp.concatenate([high, pad, low, pad], axis=0)
        split[from_slab] = right_side
        pieces = []
        for b in range(BLOCKS + 2):
            omega = maps[b, pl.ds(from_slab, 1)]
            v = maps[b, pl.ds(SLABS + from_slab, 1)]
            pieces.append(omega * away)
            pieces.append(jnp.broadcast_to(v - mean * omega, (ROWS - MEMBERS, CELLS)))
        lhs_high, lhs_low = halves(jnp.concatenate(pieces, axis=0))
        high_part = nt(lhs_high, right_side)
        low_part = nt(lhs_low, right_side[:LANES])
        total = high_part[:, :LANES] + high_part[:, LANES:] + low_part
        acc[...] += total.reshape(acc.shape)
        return carry

    lax.fori_loop(0, SLABS, gather, 0)

    def part_copy(side):
        return pltpu.make_async_remote_copy(
            src_ref=acc.at[BLOCKS + side],
            dst_ref=part_in.at[side],
            send_sem=part_send.at[side],
            recv_sem=part_recv.at[side],
            device_id=(left, right)[side],
            device_id_type=LOGICAL,
        )

    part_copy(0).start()
    part_copy(1).start()

    identity = jnp.where((spot == across) & (spot < MEMBERS), one, zero)
    empty = jnp.zeros((LANES - MEMBERS, LANES), jnp.float32)
    part_copy(0).wait_recv()
    part_copy(1).wait_recv()
    totals = [acc[b] for b in range(BLOCKS)]
    totals[BLOCKS - 1] = totals[BLOCKS - 1] + part_in[0]
    totals[0] = totals[0] + part_in[1]
    grams = [identity + jnp.concatenate([t[:MEMBERS], empty], axis=0) for t in totals]
    fros = [jnp.sqrt(jnp.sum(t * t, keepdims=True)) for t in grams]
    a_of = [t / f for t, f in zip(grams, fros)]
    middles = [1.5 * identity - 0.5 * a for a in a_of]
    z_of = middles
    a_of = [product(a, r) for a, r in zip(a_of, middles)]
    for iteration in range(1, ITERS):
        middles = [1.5 * identity - 0.5 * product(z, a) for z, a in zip(z_of, a_of)]
        if iteration < ITERS - 1:
            a_of = [product(a, r) for a, r in zip(a_of, middles)]
        z_of = [product(r, z) for r, z in zip(middles, z_of)]
    for b in range(BLOCKS):
        transform = z_of[b] * (1.0 / jnp.sqrt(fros[b]))
        projected = jnp.broadcast_to(totals[b][MEMBERS : MEMBERS + 1], (16, LANES))
        mean_weights = product(product(projected, transform), transform)[:1]
        high, low = halves(transform)
        both = nn(select[...], jnp.concatenate([high, low], axis=1))
        by_member = (both[:MEMBERS, :LANES] + both[:MEMBERS, LANES:]) + mean_weights
        high, low = halves(by_member)
        ordered[0, MEMBERS * b : MEMBERS * (b + 1)] = jnp.concatenate([high, high], axis=1)
        ordered[1, MEMBERS * b : MEMBERS * (b + 1)] = jnp.concatenate([low, low], axis=1)

    all_but_one = outgoing.at[pl.ds(0, DEVICES - 1)]
    pltpu.make_async_copy(all_but_one, all_but_one, send_sem).wait()

    block_of = (iota((MEMBERS, CELLS), 1) % OWN) // TILE_WIDTH

    def give_back(i, carry):
        to_slab = (s + i) % SLABS
        right_side = split[to_slab]
        parts = nn(ordered[0], right_side) + nn(ordered[1], right_side)
        field = parts[:MEMBERS]
        for b in range(1, BLOCKS):
            field = jnp.where(block_of == b, parts[MEMBERS * b : MEMBERS * (b + 1)], field)
        field = field + mean_of[to_slab]
        near = field[:, :LANES].reshape(12, 8, LANES)
        far = field[:, LANES:].reshape(12, 8, LANES)
        even = jnp.where(half_row, near, pltpu.roll(far, 4, 1)).reshape(4, QUADS, 8, LANES)
        odd = jnp.where(half_row, pltpu.roll(near, 4, 1), far).reshape(4, QUADS, 8, LANES)
        for a in range(4):
            incoming[GROUPS * to_slab + 2 * a] = even[a]
            incoming[GROUPS * to_slab + 2 * a + 1] = odd[a]

        def to_group(j, carry):
            peer_g = (g + j) & (GROUPS - 1)

            @pl.when(i * GROUPS + j > 0)
            def _():
                pltpu.make_async_remote_copy(
                    src_ref=incoming.at[GROUPS * to_slab + peer_g],
                    dst_ref=returned.at[me],
                    send_sem=back_send,
                    recv_sem=back_recv,
                    device_id=peer_g * SLABS + to_slab,
                    device_id_type=LOGICAL,
                ).start()

            return carry

        lax.fori_loop(0, GROUPS, to_group, 0)
        return carry

    lax.fori_loop(0, SLABS, give_back, 0)
    returned[me] = incoming[s * GROUPS + g]

    halo_copy(1).wait_send()
    back_halo.wait_send()
    back_rates.wait_send()
    for side in range(2):
        edge_copy(side).wait_send()
        part_copy(side).wait_send()
    sent = incoming.at[pl.ds(0, DEVICES - 1)]
    pltpu.make_async_copy(sent, sent, back_send).wait()
    got = returned.at[pl.ds(0, DEVICES - 1)]
    pltpu.make_async_copy(got, got, back_recv).wait()

    def unpack(tile, carry):
        for quad in range(QUADS):
            tiles = swap_lanes([returned[4 * tile + q, quad] for q in range(4)], lane)
            tiles = swap_rows(tiles, row)
            for i in range(4):
                o_ref[4 * quad + i, tile] = tiles[i]
        return carry

    lax.fori_loop(0, TILES, unpack, 0, unroll=2)


def shards(
    initial_samples,
    transport_ratios,
    assignment,
    obs_values,
    obs_error,
    sensor_easting_offset,
    obs_column,
    obs_count,
):
    members, planes, columns = initial_samples.shape

    def tiled(x):
        return jnp.transpose(x.reshape(-1, planes, TILES, LANES), (0, 2, 1, 3))

    f32 = jnp.float32
    i32 = jnp.int32
    bf16 = jnp.bfloat16
    dma = pltpu.SemaphoreType.DMA
    hbm = pl.BlockSpec(memory_space=pltpu.HBM)
    out = pl.pallas_call(
        kernel,
        name="analysis",
        out_shape=jax.ShapeDtypeStruct((members, TILES, planes, LANES), f32),
        in_specs=[hbm] * 8,
        out_specs=pl.BlockSpec(memory_space=pltpu.VMEM),
        scratch_shapes=[
            pltpu.VMEM((4 * QUADS, TILES, PLANES, LANES), f32),
            pltpu.VMEM((3, TILES, PLANES, LANES), f32),
            pltpu.VMEM((1, MEMBERS), i32),
            pltpu.VMEM((BLOCKS, OBS), f32),
            pltpu.VMEM((BLOCKS, OBS), f32),
            pltpu.VMEM((BLOCKS, OBS), i32),
            pltpu.VMEM((BLOCKS, OBS), i32),
            pltpu.VMEM((1, BLOCKS), i32),
            pltpu.VMEM((3, TILES, PLANES, LANES), f32),
            pltpu.VMEM((3, PLANES + STEPS, 16, 8, LANES), f32),
            pltpu.VMEM((2, STEPS, PLANES + 1, 17, 8, LANES), f32),
            pltpu.VMEM((STEPS, PLANES + STEPS + 1, 17, 8, LANES), f32),
            pltpu.VMEM((DEVICES, QUADS, 8, LANES), f32),
            pltpu.VMEM((DEVICES, QUADS, 8, LANES), f32),
            pltpu.VMEM((DEVICES, QUADS, 8, LANES), f32),
            pltpu.VMEM((SLABS, 2 * LANES, CELLS), bf16),
            pltpu.VMEM((SLABS, 1, CELLS), f32),
            pltpu.VMEM((BLOCKS + 2, 2 * SLABS, CELLS), f32),
            pltpu.VMEM((2, 2 * SLABS, CELLS), f32),
            pltpu.VMEM((2, 2 * SLABS, CELLS), f32),
            pltpu.VMEM((BLOCKS + 2, ROWS, LANES), f32),
            pltpu.VMEM((2, ROWS, LANES), f32),
            pltpu.VMEM((LANES, LANES), bf16),
            pltpu.VMEM((2, BLOCKS * MEMBERS, 2 * LANES), bf16),
            dma((QUADS,)),
            dma((7,)),
            dma((4,)),
            dma((4,)),
            dma((2,)),
            dma((2,)),
            dma((2,)),
            dma((2,)),
            dma,
            dma((SLABS,)),
            dma,
            dma,
        ],
        compiler_params=pltpu.CompilerParams(
            collective_id=0, has_side_effects=True, vmem_limit_bytes=56 << 20
        ),
    )(
        tiled(initial_samples),
        tiled(transport_ratios),
        assignment[None, :],
        obs_values,
        obs_error,
        sensor_easting_offset,
        obs_column,
        obs_count[None, :],
    )
    return jnp.transpose(out, (0, 2, 1, 3)).reshape(members, planes, columns)


def solution(mesh):
    placed = (
        P("group", "slab", None),
        P(None, "slab", None),
        P(),
        P(("group", "slab"), None),
        P(("group", "slab"), None),
        P(("group", "slab"), None),
        P(("group", "slab"), None),
        P(("group", "slab")),
    )
    return jax.shard_map(
        shards, mesh=mesh, in_specs=placed, out_specs=P("group", "slab", None), check_vma=False
    )
```

```python
import jax
import jax.numpy as jnp
from jax import lax
from jax.experimental import pallas as pl
from jax.experimental.pallas import tpu as pltpu
from jax.sharding import PartitionSpec as P

MEMBERS = 96
NZ = 64
STEPS = 6
TILE_WIDTH = 8
HC = 8
OBS = 512
ITERS = 8

GROUPS = 8
SLABS = 16
DEVICES = GROUPS * SLABS
PLANES = 8
TILES = 32
LANES = 128
QUADS = 3
OWN = 32
BLOCKS = 4
CELLS = PLANES * OWN
ROWS = 112
LOGICAL = pl.DeviceIdType.LOGICAL


def nt(a, b):
    return lax.dot_general(a, b, (((1,), (1,)), ((), ())), preferred_element_type=jnp.float32)


def nn(a, b):
    return lax.dot_general(a, b, (((1,), (0,)), ((), ())), preferred_element_type=jnp.float32)


def halves(a):
    high = a.astype(jnp.bfloat16)
    return high, (a - high.astype(jnp.float32)).astype(jnp.bfloat16)


def product(a, b):
    m = a.shape[0]
    ah, al = halves(a)
    bh, bl = halves(b)
    both = nn(jnp.concatenate([ah, al], axis=0), jnp.concatenate([bh, bl], axis=1))
    return both[:m, :LANES] + (both[:m, LANES:] + both[m:, :LANES])


def swap_rows(tiles, row):
    axis = tiles[0].ndim - 2
    t0, t1, t2, t3 = tiles
    up = (row & 2) == 0
    b0 = jnp.where(up, t0, pltpu.roll(t2, 2, axis))
    b2 = jnp.where(up, pltpu.roll(t0, 6, axis), t2)
    b1 = jnp.where(up, t1, pltpu.roll(t3, 2, axis))
    b3 = jnp.where(up, pltpu.roll(t1, 6, axis), t3)
    even = (row & 1) == 0
    o0 = jnp.where(even, b0, pltpu.roll(b1, 1, axis))
    o1 = jnp.where(even, pltpu.roll(b0, 7, axis), b1)
    o2 = jnp.where(even, b2, pltpu.roll(b3, 1, axis))
    o3 = jnp.where(even, pltpu.roll(b2, 7, axis), b3)
    return o0, o1, o2, o3


def swap_lanes(tiles, lane):
    axis = tiles[0].ndim - 1
    t0, t1, t2, t3 = tiles
    low = (lane & 64) == 0
    b0 = jnp.where(low, t0, pltpu.roll(t2, 64, axis))
    b2 = jnp.where(low, pltpu.roll(t0, 64, axis), t2)
    b1 = jnp.where(low, t1, pltpu.roll(t3, 64, axis))
    b3 = jnp.where(low, pltpu.roll(t1, 64, axis), t3)
    even = (lane & 32) == 0
    o0 = jnp.where(even, b0, pltpu.roll(b1, 32, axis))
    o1 = jnp.where(even, pltpu.roll(b0, 96, axis), b1)
    o2 = jnp.where(even, b2, pltpu.roll(b3, 32, axis))
    o3 = jnp.where(even, pltpu.roll(b2, 96, axis), b3)
    return o0, o1, o2, o3


def iota(shape, dim):
    return lax.broadcasted_iota(jnp.int32, shape, dim)


def transposed(tiles, row):
    axis = tiles[0].ndim - 2
    tiles = list(tiles)
    for d in (4, 2, 1):
        upper = (row & d) == 0
        for j in range(8):
            if not j & d:
                a, b = tiles[j], tiles[j + d]
                tiles[j] = jnp.where(upper, a, pltpu.roll(b, d, axis))
                tiles[j + d] = jnp.where(upper, pltpu.roll(a, 8 - d, axis), b)
    return tiles


def kernel(
    x_hbm,
    c_hbm,
    asg_hbm,
    val_hbm,
    err_hbm,
    east_hbm,
    col_hbm,
    cnt_hbm,
    o_ref,
    x_ref,
    c_ref,
    asg_ref,
    val_ref,
    err_ref,
    east_ref,
    col_ref,
    cnt_ref,
    c_next,
    rates,
    state,
    ahead,
    outgoing,
    incoming,
    returned,
    split,
    mean_of,
    maps,
    edge_out,
    edge_in,
    acc,
    part_in,
    select,
    ordered,
    x_sem,
    small_sem,
    halo_send,
    halo_recv,
    edge_send,
    edge_recv,
    part_send,
    part_recv,
    send_sem,
    recv_sem,
    back_send,
    back_recv,
    everyone,
):
    g = lax.axis_index("group")
    s = lax.axis_index("slab")
    me = g * SLABS + s
    left = (me + DEVICES - 1) % DEVICES
    right = (me + 1) % DEVICES

    rate_copy = pltpu.make_async_copy(c_hbm, c_ref, small_sem.at[0])
    rate_copy.start()

    def sample_copy(quad):
        four = pl.ds(4 * quad, 4)
        return pltpu.make_async_copy(x_hbm.at[four], x_ref.at[four], x_sem.at[quad])

    for quad in range(QUADS):
        sample_copy(quad).start()
    small_copies = [
        pltpu.make_async_copy(source, target, small_sem.at[1 + i])
        for i, (source, target) in enumerate(
            [
                (asg_hbm, asg_ref),
                (val_hbm, val_ref),
                (err_hbm, err_ref),
                (east_hbm, east_ref),
                (col_hbm, col_ref),
                (cnt_hbm, cnt_ref),
            ]
        )
    ]
    for copy in small_copies:
        copy.start()

    barrier = pltpu.get_barrier_semaphore()

    def group_peer(i):
        return ((g + i) & (GROUPS - 1)) * SLABS + s

    def slab_peer(i):
        return g * SLABS + ((s + i) & (SLABS - 1))

    for i in range(1, SLABS):
        pl.semaphore_signal(
            barrier, inc=1, device_id=slab_peer(i), device_id_type=LOGICAL
        )
    for i in range(1, GROUPS):
        pl.semaphore_signal(
            barrier, inc=1, device_id=group_peer(i), device_id_type=LOGICAL
        )

    row = iota((8, LANES), 0)
    lane = iota((8, LANES), 1)
    upper_half = row < 4
    low_half = lane < 64
    z_first = (lane & (NZ - 1)) == 0

    def lanes_swapped(a, b):
        first = jnp.where(low_half, a, pltpu.roll(b, 64, 1))
        second = jnp.where(low_half, pltpu.roll(a, 64, 1), b)
        return jnp.stack([first, second])

    rate_copy.wait()

    def take_rates(source, planes, offset):
        def one(u, carry):
            for i in range(3):
                sides = [
                    lanes_swapped(source[i, u + 16 * h], source[i, u + 16 * h + 8])
                    for h in range(2)
                ]
                for x in range(planes):
                    rates[i, offset + x, pl.ds(2 * u, 2)] = jnp.where(
                        upper_half, sides[0][:, x : x + 1], sides[1][:, x : x + 1]
                    )
            return carry

        lax.fori_loop(0, 8, one, 0)

    take_rates(c_ref, PLANES, 0)

    def wrap(grid, level, first, end):
        last = grid[level, first + 1 : end + 1, 16]
        turned = pltpu.roll(last, 64, 2)
        grid[level, first + 1 : end + 1, 0] = jnp.where(
            low_half, pltpu.roll(turned, 4, 1), turned
        )

    def take_samples(quad, grid):
        sample_copy(quad).wait()

        def one(u, carry):
            tiles = []
            for h in range(2):
                for i in range(4):
                    at = 4 * quad + i
                    tiles.append(lanes_swapped(x_ref[at, u + 16 * h], x_ref[at, u + 16 * h + 8]))
            for x, tile in enumerate(transposed(tiles, row)):
                grid[0, x + 1, pl.ds(2 * u + 1, 2)] = tile
            return carry

        lax.fori_loop(0, 8, one, 0)
        wrap(grid, 0, 0, PLANES)

    def stepped(grid, level, first, end, ty, n):
        u = grid[level, first + 1 : end + 1, pl.ds(ty + 1, n)]
        above = grid[level, first:end, pl.ds(ty + 1, n)]
        below_y = grid[level, first + 1 : end + 1, pl.ds(ty, n)]
        below_z = jnp.where(z_first, pltpu.roll(u, 65, 3), pltpu.roll(u, 1, 3))
        return (
            u
            - rates[0, first:end, pl.ds(ty, n)] * (u - above)
            - rates[1, first:end, pl.ds(ty, n)] * (u - below_y)
            - rates[2, first:end, pl.ds(ty, n)] * (u - below_z)
        )

    def advance(grid, level, first, end):
        planes = end - first
        n = 16 if planes < 3 else 8 if planes < 6 else 4

        def one(i, carry):
            new = stepped(grid, level, first, end, n * i, n)
            grid[level + 1, first + 1 : end + 1, pl.ds(n * i + 1, n)] = new
            return carry

        lax.fori_loop(0, 16 // n, one, 0)
        wrap(grid, level + 1, first, end)

    next_slab = g * SLABS + ((s + 1) & (SLABS - 1))
    last_slab = g * SLABS + ((s + SLABS - 1) & (SLABS - 1))

    def halo_copy(quad):
        return pltpu.make_async_remote_copy(
            src_ref=state.at[quad, :, PLANES, pl.ds(1, 16)],
            dst_ref=state.at[quad, :, 0, pl.ds(1, 16)],
            send_sem=halo_send.at[quad],
            recv_sem=halo_recv.at[quad],
            device_id=next_slab,
            device_id_type=LOGICAL,
        )

    back_halo = pltpu.make_async_remote_copy(
        src_ref=ahead.at[0, pl.ds(1, STEPS), pl.ds(1, 16)],
        dst_ref=ahead.at[0, pl.ds(PLANES + 1, STEPS), pl.ds(1, 16)],
        send_sem=halo_send.at[2],
        recv_sem=halo_recv.at[2],
        device_id=last_slab,
        device_id_type=LOGICAL,
    )
    back_rates = pltpu.make_async_remote_copy(
        src_ref=c_ref,
        dst_ref=c_next,
        send_sem=halo_send.at[3],
        recv_sem=halo_recv.at[3],
        device_id=last_slab,
        device_id_type=LOGICAL,
    )

    grids = [state.at[0], state.at[1]]

    def own_cone(quad):
        take_samples(quad, grids[quad])
        for level in range(STEPS - 1):
            advance(grids[quad], level, level + 3, PLANES)

    own_cone(0)
    pl.semaphore_wait(barrier, SLABS + GROUPS - 2)
    halo_copy(0).start()
    back_rates.start()
    for i in range(1, GROUPS):
        pl.semaphore_signal(everyone, inc=1, device_id=group_peer(i), device_id_type=LOGICAL)
    take_samples(2, ahead)
    back_halo.start()
    own_cone(1)
    for level in range(STEPS - 1):
        advance(ahead, level, level + 1, PLANES)

    for copy in small_copies:
        copy.wait()

    slots = iota((1, OBS), 1)
    for b in range(BLOCKS):
        live = slots < cnt_ref[:, b : b + 1]
        square = jnp.where(live, 1.0 / (err_ref[b : b + 1, :] * (MEMBERS - 1.0)), 0.0)
        valued = square * val_ref[b : b + 1, :]
        easting = east_ref[b : b + 1, :]
        column = TILE_WIDTH * b - HC + col_ref[b : b + 1, :]
        at_slab = iota((SLABS, OBS), 0) == (easting >> 3)
        left_side = jnp.concatenate(
            [jnp.where(at_slab, square, 0.0), jnp.where(at_slab, valued, 0.0)], axis=0
        )
        high, low = halves(left_side)
        both = jnp.concatenate([high, low], axis=0)
        cell = iota((CELLS, OBS), 0)
        base = (easting & (PLANES - 1)) * OWN

        def spread(inside, offset):
            at = jnp.where(inside, base + column + offset, -1)
            hot = jnp.where(cell == at, 1.0, 0.0).astype(jnp.bfloat16)
            got = nt(both, hot)
            return got[: 2 * SLABS] + got[2 * SLABS :]

        maps[b] = spread((column >= 0) & (column < OWN), 0)
        if b == 0:
            edge_out[0] = spread(column < 0, OWN)
        if b == BLOCKS - 1:
            edge_out[1] = spread(column >= OWN, -OWN)

    def edge_copy(side):
        return pltpu.make_async_remote_copy(
            src_ref=edge_out.at[side],
            dst_ref=edge_in.at[side],
            send_sem=edge_send.at[side],
            recv_sem=edge_recv.at[side],
            device_id=(left, right)[side],
            device_id_type=LOGICAL,
        )

    pl.semaphore_wait(everyone, GROUPS - 1)
    edge_copy(0).start()
    edge_copy(1).start()

    spot = iota((LANES, LANES), 0)
    across = iota((LANES, LANES), 1)

    def member(r):
        return 24 * (r // 24) + 12 * ((r // 4) % 2) + 4 * ((r // 8) % 3) + r % 4

    one = jnp.float32(1.0)
    zero = jnp.float32(0.0)
    slot_lane = iota((LANES, MEMBERS), 1)
    slot_spot = iota((LANES, MEMBERS), 0)
    hot = jnp.where(asg_ref[...] == slot_spot, one, zero).astype(jnp.bfloat16)
    order = jnp.where((member(spot) == across) & (spot < MEMBERS), one, zero).astype(jnp.bfloat16)
    slot_order = jnp.where((member(slot_spot) == slot_lane) & (slot_spot < MEMBERS), one, zero)
    member_rows = nn(order, hot).astype(jnp.bfloat16)
    select[...] = nt(member_rows, slot_order.astype(jnp.bfloat16)).astype(jnp.bfloat16)

    def send_all(quad):
        def send(k, carry):
            peer = (((g + (k >> 4)) & (GROUPS - 1)) * SLABS) + ((s + k) & (SLABS - 1))
            pltpu.make_async_remote_copy(
                src_ref=outgoing.at[peer, quad],
                dst_ref=incoming.at[s * GROUPS + g, quad],
                send_sem=send_sem,
                recv_sem=recv_sem.at[s],
                device_id=peer,
                device_id_type=LOGICAL,
            ).start()
            return carry

        lax.fori_loop(1, DEVICES, send, 0, unroll=2)

    def pack_all(quad, grid, first):
        def pack(i, carry):
            ty = 4 * i
            new = stepped(grid, STEPS - 1, first, first + PLANES, ty, 4)
            at_plane = [new[(x - first) % PLANES] for x in range(PLANES)]
            for h in range(2):
                tiles = []
                for x in range(4):
                    a, b = at_plane[x], at_plane[4 + x]
                    if h == 0:
                        tiles.append(jnp.where(upper_half, a, pltpu.roll(b, 4, 1)))
                    else:
                        tiles.append(jnp.where(upper_half, pltpu.roll(a, 4, 1), b))
                for j, tile in enumerate(swap_lanes(tiles, lane)):
                    for k in range(4):
                        at = 64 * h + 32 * (j // 2) + 2 * k + j % 2
                        outgoing[at + 2 * ty, quad] = tile[k]
            return carry

        lax.fori_loop(0, 4, pack, 0)

    def forecast(quad):
        halo_copy(quad).wait_recv()
        for level in range(STEPS - 1):
            advance(grids[quad], level, 0, level + 3)
        pack_all(quad, grids[quad], 0)

    halo_copy(0).wait_send()
    halo_copy(1).start()
    forecast(0)
    send_all(0)
    back_rates.wait_recv()
    take_rates(c_next, STEPS, PLANES)
    back_halo.wait_recv()
    wrap(ahead, 0, PLANES, PLANES + STEPS)
    for level in range(STEPS - 1):
        advance(ahead, level, PLANES, PLANES + STEPS)
    pack_all(2, ahead, STEPS)
    send_all(2)
    forecast(1)
    send_all(1)

    incoming[s * GROUPS + g] = outgoing[me]

    edge_copy(0).wait_recv()
    edge_copy(1).wait_recv()
    maps[BLOCKS] = edge_in[1]
    maps[BLOCKS + 1] = edge_in[0]
    acc[...] = jnp.zeros(acc.shape, jnp.float32)

    half_row = iota((12, 8, LANES), 1) < 4
    pad = jnp.zeros((LANES - MEMBERS, CELLS), jnp.bfloat16)

    late = (iota((GROUPS, 8, LANES), 1) >= 4) & (iota((GROUPS, 8, LANES), 2) >= 64)
    seven = incoming.at[pl.ds(0, GROUPS - 1)]
    pltpu.make_async_copy(seven, seven, recv_sem.at[s]).wait()

    def gather(i, carry):
        from_slab = (s - i) & (SLABS - 1)
        before = (s - i - 1) & (SLABS - 1)

        @pl.when(i < SLABS - 1)
        def _():
            eight = incoming.at[pl.ds(0, GROUPS)]
            pltpu.make_async_copy(eight, eight, recv_sem.at[before]).wait()

        got = incoming[pl.ds(GROUPS * from_slab, GROUPS)]
        third = jnp.where(late, got[:, 2], incoming[pl.ds(GROUPS * before, GROUPS), 2])
        got = jnp.concatenate([got[:, :2], third[:, None]], axis=1).reshape(4, 2, QUADS, 8, LANES)
        a = got[:, 0].reshape(12, 8, LANES)
        b = got[:, 1].reshape(12, 8, LANES)
        near = jnp.where(half_row, a, pltpu.roll(b, 4, 1)).reshape(MEMBERS, LANES)
        far = jnp.where(half_row, pltpu.roll(a, 4, 1), b).reshape(MEMBERS, LANES)
        field = jnp.concatenate([near, far], axis=1)
        mean = jnp.sum(field, axis=0, keepdims=True) * (1.0 / MEMBERS)
        mean_of[from_slab] = mean
        away = field - mean
        high, low = halves(away)
        right_side = jnp.concatenate([high, pad, low, pad], axis=0)
        split[from_slab] = right_side
        pieces = []
        for b in range(BLOCKS + 2):
            omega = maps[b, pl.ds(from_slab, 1)]
            v = maps[b, pl.ds(SLABS + from_slab, 1)]
            pieces.append(omega * away)
            pieces.append(jnp.broadcast_to(v - mean * omega, (ROWS - MEMBERS, CELLS)))
        lhs_high, lhs_low = halves(jnp.concatenate(pieces, axis=0))
        high_part = nt(lhs_high, right_side)
        low_part = nt(lhs_low, right_side[:LANES])
        total = high_part[:, :LANES] + high_part[:, LANES:] + low_part
        acc[...] += total.reshape(acc.shape)
        return carry

    lax.fori_loop(0, SLABS, gather, 0)

    def part_copy(side):
        return pltpu.make_async_remote_copy(
            src_ref=acc.at[BLOCKS + side],
            dst_ref=part_in.at[side],
            send_sem=part_send.at[side],
            recv_sem=part_recv.at[side],
            device_id=(left, right)[side],
            device_id_type=LOGICAL,
        )

    part_copy(0).start()
    part_copy(1).start()

    identity = jnp.where((spot == across) & (spot < MEMBERS), one, zero)
    empty = jnp.zeros((LANES - MEMBERS, LANES), jnp.float32)
    part_copy(0).wait_recv()
    part_copy(1).wait_recv()
    totals = [acc[b] for b in range(BLOCKS)]
    totals[BLOCKS - 1] = totals[BLOCKS - 1] + part_in[0]
    totals[0] = totals[0] + part_in[1]
    grams = [identity + jnp.concatenate([t[:MEMBERS], empty], axis=0) for t in totals]
    fros = [jnp.sqrt(jnp.sum(t * t, keepdims=True)) for t in grams]
    a_of = [t / f for t, f in zip(grams, fros)]
    middles = [1.5 * identity - 0.5 * a for a in a_of]
    z_of = middles
    a_of = [product(a, r) for a, r in zip(a_of, middles)]
    for iteration in range(1, ITERS):
        middles = [1.5 * identity - 0.5 * product(z, a) for z, a in zip(z_of, a_of)]
        if iteration < ITERS - 1:
            a_of = [product(a, r) for a, r in zip(a_of, middles)]
        z_of = [product(r, z) for r, z in zip(middles, z_of)]
    for b in range(BLOCKS):
        transform = z_of[b] * (1.0 / jnp.sqrt(fros[b]))
        projected = jnp.broadcast_to(totals[b][MEMBERS : MEMBERS + 1], (16, LANES))
        mean_weights = product(product(projected, transform), transform)[:1]
        high, low = halves(transform)
        both = nn(select[...], jnp.concatenate([high, low], axis=1))
        by_member = (both[:MEMBERS, :LANES] + both[:MEMBERS, LANES:]) + mean_weights
        high, low = halves(by_member)
        ordered[0, MEMBERS * b : MEMBERS * (b + 1)] = jnp.concatenate([high, high], axis=1)
        ordered[1, MEMBERS * b : MEMBERS * (b + 1)] = jnp.concatenate([low, low], axis=1)

    all_but_one = outgoing.at[pl.ds(0, DEVICES - 1)]
    pltpu.make_async_copy(all_but_one, all_but_one, send_sem).wait()

    block_of = (iota((MEMBERS, CELLS), 1) % OWN) // TILE_WIDTH

    def give_back(i, carry):
        to_slab = (s + i) % SLABS
        right_side = split[to_slab]
        parts = nn(ordered[0], right_side) + nn(ordered[1], right_side)
        field = parts[:MEMBERS]
        for b in range(1, BLOCKS):
            field = jnp.where(block_of == b, parts[MEMBERS * b : MEMBERS * (b + 1)], field)
        field = field + mean_of[to_slab]
        near = field[:, :LANES].reshape(12, 8, LANES)
        far = field[:, LANES:].reshape(12, 8, LANES)
        even = jnp.where(half_row, near, pltpu.roll(far, 4, 1)).reshape(4, QUADS, 8, LANES)
        odd = jnp.where(half_row, pltpu.roll(near, 4, 1), far).reshape(4, QUADS, 8, LANES)
        for a in range(4):
            incoming[GROUPS * to_slab + 2 * a] = even[a]
            incoming[GROUPS * to_slab + 2 * a + 1] = odd[a]

        def to_group(j, carry):
            peer_g = (g + j) & (GROUPS - 1)

            @pl.when(i * GROUPS + j > 0)
            def _():
                pltpu.make_async_remote_copy(
                    src_ref=incoming.at[GROUPS * to_slab + peer_g],
                    dst_ref=returned.at[me],
                    send_sem=back_send,
                    recv_sem=back_recv,
                    device_id=peer_g * SLABS + to_slab,
                    device_id_type=LOGICAL,
                ).start()

            return carry

        lax.fori_loop(0, GROUPS, to_group, 0)
        return carry

    lax.fori_loop(0, SLABS, give_back, 0)
    returned[me] = incoming[s * GROUPS + g]

    halo_copy(1).wait_send()
    back_halo.wait_send()
    back_rates.wait_send()
    for side in range(2):
        edge_copy(side).wait_send()
        part_copy(side).wait_send()
    sent = incoming.at[pl.ds(0, DEVICES - 1)]
    pltpu.make_async_copy(sent, sent, back_send).wait()
    got = returned.at[pl.ds(0, DEVICES - 1)]
    pltpu.make_async_copy(got, got, back_recv).wait()

    def unpack(tile, carry):
        for quad in range(QUADS):
            tiles = swap_lanes([returned[4 * tile + q, quad] for q in range(4)], lane)
            tiles = swap_rows(tiles, row)
            for i in range(4):
                o_ref[4 * quad + i, tile] = tiles[i]
        return carry

    lax.fori_loop(0, TILES, unpack, 0, unroll=2)


def shards(
    initial_samples,
    transport_ratios,
    assignment,
    obs_values,
    obs_error,
    sensor_easting_offset,
    obs_column,
    obs_count,
):
    members, planes, columns = initial_samples.shape

    def tiled(x):
        return jnp.transpose(x.reshape(-1, planes, TILES, LANES), (0, 2, 1, 3))

    f32 = jnp.float32
    i32 = jnp.int32
    bf16 = jnp.bfloat16
    dma = pltpu.SemaphoreType.DMA
    hbm = pl.BlockSpec(memory_space=pltpu.HBM)
    out = pl.pallas_call(
        kernel,
        name="analysis",
        out_shape=jax.ShapeDtypeStruct((members, TILES, planes, LANES), f32),
        in_specs=[hbm] * 8,
        out_specs=pl.BlockSpec(memory_space=pltpu.VMEM),
        scratch_shapes=[
            pltpu.VMEM((4 * QUADS, TILES, PLANES, LANES), f32),
            pltpu.VMEM((3, TILES, PLANES, LANES), f32),
            pltpu.VMEM((1, MEMBERS), i32),
            pltpu.VMEM((BLOCKS, OBS), f32),
            pltpu.VMEM((BLOCKS, OBS), f32),
            pltpu.VMEM((BLOCKS, OBS), i32),
            pltpu.VMEM((BLOCKS, OBS), i32),
            pltpu.VMEM((1, BLOCKS), i32),
            pltpu.VMEM((3, TILES, PLANES, LANES), f32),
            pltpu.VMEM((3, PLANES + STEPS, 16, 8, LANES), f32),
            pltpu.VMEM((2, STEPS, PLANES + 1, 17, 8, LANES), f32),
            pltpu.VMEM((STEPS, PLANES + STEPS + 1, 17, 8, LANES), f32),
            pltpu.VMEM((DEVICES, QUADS, 8, LANES), f32),
            pltpu.VMEM((DEVICES, QUADS, 8, LANES), f32),
            pltpu.VMEM((DEVICES, QUADS, 8, LANES), f32),
            pltpu.VMEM((SLABS, 2 * LANES, CELLS), bf16),
            pltpu.VMEM((SLABS, 1, CELLS), f32),
            pltpu.VMEM((BLOCKS + 2, 2 * SLABS, CELLS), f32),
            pltpu.VMEM((2, 2 * SLABS, CELLS), f32),
            pltpu.VMEM((2, 2 * SLABS, CELLS), f32),
            pltpu.VMEM((BLOCKS + 2, ROWS, LANES), f32),
            pltpu.VMEM((2, ROWS, LANES), f32),
            pltpu.VMEM((LANES, LANES), bf16),
            pltpu.VMEM((2, BLOCKS * MEMBERS, 2 * LANES), bf16),
            dma((QUADS,)),
            dma((7,)),
            dma((4,)),
            dma((4,)),
            dma((2,)),
            dma((2,)),
            dma((2,)),
            dma((2,)),
            dma,
            dma((SLABS,)),
            dma,
            dma,
            pltpu.SemaphoreType.REGULAR,
        ],
        compiler_params=pltpu.CompilerParams(
            collective_id=0, has_side_effects=True, vmem_limit_bytes=56 << 20
        ),
    )(
        tiled(initial_samples),
        tiled(transport_ratios),
        assignment[None, :],
        obs_values,
        obs_error,
        sensor_easting_offset,
        obs_column,
        obs_count[None, :],
    )
    return jnp.transpose(out, (0, 2, 1, 3)).reshape(members, planes, columns)


def solution(mesh):
    placed = (
        P("group", "slab", None),
        P(None, "slab", None),
        P(),
        P(("group", "slab"), None),
        P(("group", "slab"), None),
        P(("group", "slab"), None),
        P(("group", "slab"), None),
        P(("group", "slab")),
    )
    return jax.shard_map(
        shards, mesh=mesh, in_specs=placed, out_specs=P("group", "slab", None), check_vma=False
    )
```

```python
import jax
import jax.numpy as jnp
from jax import lax
from jax.experimental import pallas as pl
from jax.experimental.pallas import tpu as pltpu
from jax.sharding import PartitionSpec as P

MEMBERS = 96
NZ = 64
STEPS = 6
TILE_WIDTH = 8
HC = 8
OBS = 512
ITERS = 8

GROUPS = 8
SLABS = 16
DEVICES = GROUPS * SLABS
PLANES = 8
TILES = 32
LANES = 128
QUADS = 3
OWN = 32
BLOCKS = 4
CELLS = PLANES * OWN
ROWS = 112
LOGICAL = pl.DeviceIdType.LOGICAL


def nt(a, b):
    return lax.dot_general(a, b, (((1,), (1,)), ((), ())), preferred_element_type=jnp.float32)


def nn(a, b):
    return lax.dot_general(a, b, (((1,), (0,)), ((), ())), preferred_element_type=jnp.float32)


def halves(a):
    high = a.astype(jnp.bfloat16)
    return high, (a - high.astype(jnp.float32)).astype(jnp.bfloat16)


def padded(a):
    return jnp.concatenate([a, jnp.zeros((LANES - MEMBERS, LANES), a.dtype)], axis=0)


def product(a, b):
    ah, al = halves(a)
    bh, bl = halves(b)
    bh, bl = padded(bh), padded(bl)
    top = jnp.concatenate([bh, bl], axis=1)
    bottom = jnp.concatenate([bh, jnp.zeros_like(bl)], axis=1)
    both = nn(jnp.concatenate([ah, al], axis=1), jnp.concatenate([top, bottom], axis=0))
    return both[:, :LANES] + both[:, LANES:]


def swap_rows(tiles, row):
    axis = tiles[0].ndim - 2
    t0, t1, t2, t3 = tiles
    up = (row & 2) == 0
    b0 = jnp.where(up, t0, pltpu.roll(t2, 2, axis))
    b2 = jnp.where(up, pltpu.roll(t0, 6, axis), t2)
    b1 = jnp.where(up, t1, pltpu.roll(t3, 2, axis))
    b3 = jnp.where(up, pltpu.roll(t1, 6, axis), t3)
    even = (row & 1) == 0
    o0 = jnp.where(even, b0, pltpu.roll(b1, 1, axis))
    o1 = jnp.where(even, pltpu.roll(b0, 7, axis), b1)
    o2 = jnp.where(even, b2, pltpu.roll(b3, 1, axis))
    o3 = jnp.where(even, pltpu.roll(b2, 7, axis), b3)
    return o0, o1, o2, o3


def swap_lanes(tiles, lane):
    axis = tiles[0].ndim - 1
    t0, t1, t2, t3 = tiles
    low = (lane & 64) == 0
    b0 = jnp.where(low, t0, pltpu.roll(t2, 64, axis))
    b2 = jnp.where(low, pltpu.roll(t0, 64, axis), t2)
    b1 = jnp.where(low, t1, pltpu.roll(t3, 64, axis))
    b3 = jnp.where(low, pltpu.roll(t1, 64, axis), t3)
    even = (lane & 32) == 0
    o0 = jnp.where(even, b0, pltpu.roll(b1, 32, axis))
    o1 = jnp.where(even, pltpu.roll(b0, 96, axis), b1)
    o2 = jnp.where(even, b2, pltpu.roll(b3, 32, axis))
    o3 = jnp.where(even, pltpu.roll(b2, 96, axis), b3)
    return o0, o1, o2, o3


def iota(shape, dim):
    return lax.broadcasted_iota(jnp.int32, shape, dim)


def transposed(tiles, row):
    axis = tiles[0].ndim - 2
    tiles = list(tiles)
    for d in (4, 2, 1):
        upper = (row & d) == 0
        for j in range(8):
            if not j & d:
                a, b = tiles[j], tiles[j + d]
                tiles[j] = jnp.where(upper, a, pltpu.roll(b, d, axis))
                tiles[j + d] = jnp.where(upper, pltpu.roll(a, 8 - d, axis), b)
    return tiles


def kernel(
    x_hbm,
    c_hbm,
    asg_hbm,
    val_hbm,
    err_hbm,
    east_hbm,
    col_hbm,
    cnt_hbm,
    o_ref,
    x_ref,
    c_ref,
    asg_ref,
    val_ref,
    err_ref,
    east_ref,
    col_ref,
    cnt_ref,
    c_next,
    rates,
    state,
    ahead,
    outgoing,
    incoming,
    returned,
    split,
    mean_of,
    maps,
    edge_out,
    edge_in,
    acc,
    part_in,
    select,
    ordered,
    x_sem,
    small_sem,
    halo_send,
    halo_recv,
    edge_send,
    edge_recv,
    part_send,
    part_recv,
    send_sem,
    early_sem,
    recv_sem,
    back_send,
    back_recv,
    everyone,
):
    g = lax.axis_index("group")
    s = lax.axis_index("slab")
    me = g * SLABS + s
    left = (me + DEVICES - 1) % DEVICES
    right = (me + 1) % DEVICES

    rate_copy = pltpu.make_async_copy(c_hbm, c_ref, small_sem.at[0])
    rate_copy.start()

    def sample_copy(quad):
        four = pl.ds(4 * quad, 4)
        return pltpu.make_async_copy(x_hbm.at[four], x_ref.at[four], x_sem.at[quad])

    for quad in range(QUADS):
        sample_copy(quad).start()
    small_copies = [
        pltpu.make_async_copy(source, target, small_sem.at[1 + i])
        for i, (source, target) in enumerate(
            [
                (asg_hbm, asg_ref),
                (val_hbm, val_ref),
                (err_hbm, err_ref),
                (east_hbm, east_ref),
                (col_hbm, col_ref),
                (cnt_hbm, cnt_ref),
            ]
        )
    ]
    for copy in small_copies:
        copy.start()

    barrier = pltpu.get_barrier_semaphore()

    def group_peer(i):
        return ((g + i) & (GROUPS - 1)) * SLABS + s

    def slab_peer(i):
        return g * SLABS + ((s + i) & (SLABS - 1))

    for i in range(1, SLABS):
        pl.semaphore_signal(
            barrier, inc=1, device_id=slab_peer(i), device_id_type=LOGICAL
        )
    for i in range(1, GROUPS):
        pl.semaphore_signal(
            barrier, inc=1, device_id=group_peer(i), device_id_type=LOGICAL
        )

    row = iota((8, LANES), 0)
    lane = iota((8, LANES), 1)
    upper_half = row < 4
    low_half = lane < 64
    z_first = (lane & (NZ - 1)) == 0

    def lanes_swapped(a, b):
        first = jnp.where(low_half, a, pltpu.roll(b, 64, 1))
        second = jnp.where(low_half, pltpu.roll(a, 64, 1), b)
        return jnp.stack([first, second])

    rate_copy.wait()

    def take_rates(source, planes, offset):
        def one(u, carry):
            for i in range(3):
                sides = [
                    lanes_swapped(source[i, u + 16 * h], source[i, u + 16 * h + 8])
                    for h in range(2)
                ]
                for x in range(planes):
                    rates[i, offset + x, pl.ds(2 * u, 2)] = jnp.where(
                        upper_half, sides[0][:, x : x + 1], sides[1][:, x : x + 1]
                    )
            return carry

        lax.fori_loop(0, 8, one, 0)

    take_rates(c_ref, PLANES, 0)

    def wrap(grid, level, first, end):
        last = grid[level, first + 1 : end + 1, 16]
        turned = pltpu.roll(last, 64, 2)
        grid[level, first + 1 : end + 1, 0] = jnp.where(
            low_half, pltpu.roll(turned, 4, 1), turned
        )

    def take_samples(quad, grid):
        sample_copy(quad).wait()

        def one(u, carry):
            tiles = []
            for h in range(2):
                for i in range(4):
                    at = 4 * quad + i
                    tiles.append(lanes_swapped(x_ref[at, u + 16 * h], x_ref[at, u + 16 * h + 8]))
            for x, tile in enumerate(transposed(tiles, row)):
                grid[0, x + 1, pl.ds(2 * u + 1, 2)] = tile
            return carry

        lax.fori_loop(0, 8, one, 0)
        wrap(grid, 0, 0, PLANES)

    def stepped(grid, level, first, end, ty, n):
        u = grid[level, first + 1 : end + 1, pl.ds(ty + 1, n)]
        above = grid[level, first:end, pl.ds(ty + 1, n)]
        below_y = grid[level, first + 1 : end + 1, pl.ds(ty, n)]
        below_z = jnp.where(z_first, pltpu.roll(u, 65, 3), pltpu.roll(u, 1, 3))
        return (
            u
            - rates[0, first:end, pl.ds(ty, n)] * (u - above)
            - rates[1, first:end, pl.ds(ty, n)] * (u - below_y)
            - rates[2, first:end, pl.ds(ty, n)] * (u - below_z)
        )

    def advance(grid, level, first, end):
        planes = end - first
        n = 16 if planes < 3 else 8 if planes < 6 else 4

        def one(i, carry):
            new = stepped(grid, level, first, end, n * i, n)
            grid[level + 1, first + 1 : end + 1, pl.ds(n * i + 1, n)] = new
            return carry

        lax.fori_loop(0, 16 // n, one, 0)
        wrap(grid, level + 1, first, end)

    next_slab = g * SLABS + ((s + 1) & (SLABS - 1))
    last_slab = g * SLABS + ((s + SLABS - 1) & (SLABS - 1))

    def halo_copy(quad, low, high, sem):
        levels = pl.ds(low, high - low)
        return pltpu.make_async_remote_copy(
            src_ref=state.at[quad, levels, PLANES, pl.ds(1, 16)],
            dst_ref=state.at[quad, levels, 0, pl.ds(1, 16)],
            send_sem=halo_send.at[sem],
            recv_sem=halo_recv.at[sem],
            device_id=next_slab,
            device_id_type=LOGICAL,
        )

    halo_0 = halo_copy(0, 0, STEPS, 0)
    halo_1a = halo_copy(1, 0, 3, 1)
    halo_1b = halo_copy(1, 3, STEPS, 2)

    back_halo = pltpu.make_async_remote_copy(
        src_ref=ahead.at[0, pl.ds(1, STEPS), pl.ds(1, 16)],
        dst_ref=ahead.at[0, pl.ds(PLANES + 1, STEPS), pl.ds(1, 16)],
        send_sem=halo_send.at[3],
        recv_sem=halo_recv.at[3],
        device_id=last_slab,
        device_id_type=LOGICAL,
    )
    half = pl.ds((g & 1) * (TILES // 2), TILES // 2)
    back_rates = pltpu.make_async_remote_copy(
        src_ref=c_ref.at[:, half],
        dst_ref=c_next.at[:, half],
        send_sem=halo_send.at[4],
        recv_sem=halo_recv.at[4],
        device_id=last_slab,
        device_id_type=LOGICAL,
    )
    share_rates = pltpu.make_async_remote_copy(
        src_ref=c_next.at[:, half],
        dst_ref=c_next.at[:, half],
        send_sem=halo_send.at[5],
        recv_sem=halo_recv.at[5],
        device_id=(g ^ 1) * SLABS + s,
        device_id_type=LOGICAL,
    )

    grids = [state.at[0], state.at[1]]

    def own_cone(quad):
        take_samples(quad, grids[quad])
        for level in range(STEPS - 1):
            advance(grids[quad], level, level + 3, PLANES)

    own_cone(0)
    pl.semaphore_wait(barrier, SLABS + GROUPS - 2)
    halo_0.start()
    back_rates.start()
    for i in range(1, GROUPS):
        pl.semaphore_signal(everyone, inc=1, device_id=group_peer(i), device_id_type=LOGICAL)
    take_samples(2, ahead)
    back_halo.start()
    own_cone(1)
    halo_1a.start()
    for level in range(STEPS - 1):
        advance(ahead, level, level + 1, PLANES)
    back_rates.wait_recv()
    share_rates.start()

    for copy in small_copies:
        copy.wait()

    slots = iota((1, OBS), 1)
    for b in range(BLOCKS):
        live = slots < cnt_ref[:, b : b + 1]
        square = jnp.where(live, 1.0 / (err_ref[b : b + 1, :] * (MEMBERS - 1.0)), 0.0)
        valued = square * val_ref[b : b + 1, :]
        easting = east_ref[b : b + 1, :]
        column = TILE_WIDTH * b - HC + col_ref[b : b + 1, :]
        at_slab = iota((SLABS, OBS), 0) == (easting >> 3)
        left_side = jnp.concatenate(
            [jnp.where(at_slab, square, 0.0), jnp.where(at_slab, valued, 0.0)], axis=0
        )
        high, low = halves(left_side)
        both = jnp.concatenate([high, low], axis=0)
        cell = iota((CELLS, OBS), 0)
        base = (easting & (PLANES - 1)) * OWN

        def spread(inside, offset):
            at = jnp.where(inside, base + column + offset, -1)
            hot = jnp.where(cell == at, 1.0, 0.0).astype(jnp.bfloat16)
            got = nt(both, hot)
            return got[: 2 * SLABS] + got[2 * SLABS :]

        maps[b] = spread((column >= 0) & (column < OWN), 0)
        if b == 0:
            edge_out[0] = spread(column < 0, OWN)
        if b == BLOCKS - 1:
            edge_out[1] = spread(column >= OWN, -OWN)

    def edge_copy(side):
        return pltpu.make_async_remote_copy(
            src_ref=edge_out.at[side],
            dst_ref=edge_in.at[side],
            send_sem=edge_send.at[side],
            recv_sem=edge_recv.at[side],
            device_id=(left, right)[side],
            device_id_type=LOGICAL,
        )

    pl.semaphore_wait(everyone, GROUPS - 1)
    edge_copy(0).start()
    edge_copy(1).start()

    spot = iota((LANES, LANES), 0)
    across = iota((LANES, LANES), 1)

    def member(r):
        return 24 * (r // 24) + 12 * ((r // 4) % 2) + 4 * ((r // 8) % 3) + r % 4

    one = jnp.float32(1.0)
    zero = jnp.float32(0.0)
    slot_lane = iota((LANES, MEMBERS), 1)
    slot_spot = iota((LANES, MEMBERS), 0)
    hot = jnp.where(asg_ref[...] == slot_spot, one, zero).astype(jnp.bfloat16)
    order = jnp.where((member(spot) == across) & (spot < MEMBERS), one, zero).astype(jnp.bfloat16)
    slot_order = jnp.where((member(slot_spot) == slot_lane) & (slot_spot < MEMBERS), one, zero)
    member_rows = nn(order, hot).astype(jnp.bfloat16)
    select[...] = nt(member_rows, slot_order.astype(jnp.bfloat16)).astype(jnp.bfloat16)

    def send_all(quad):
        def send(k, carry):
            peer = (((g + (k >> 4)) & (GROUPS - 1)) * SLABS) + ((s + k) & (SLABS - 1))
            pltpu.make_async_remote_copy(
                src_ref=outgoing.at[peer, quad],
                dst_ref=incoming.at[s * GROUPS + g, quad],
                send_sem=send_sem.at[quad],
                recv_sem=early_sem.at[quad],
                device_id=peer,
                device_id_type=LOGICAL,
            ).start()
            return carry

        lax.fori_loop(1, DEVICES, send, 0, unroll=2)

    def slab_of(i, c, sign):
        z = (s >> 2) + sign * (c + i)
        y = s + sign * c
        return ((z & 3) << 2) | (y & 3)

    def send_last(k, carry):
        peer_g = (g + (k >> 2) + 2 * k) & (GROUPS - 1)
        peer_s = slab_of(k >> 5, k & 3, 1)
        peer = peer_g * SLABS + peer_s
        pltpu.make_async_remote_copy(
            src_ref=outgoing.at[peer, 1],
            dst_ref=incoming.at[s * GROUPS + g, 1],
            send_sem=send_sem.at[1],
            recv_sem=recv_sem.at[s],
            device_id=peer,
            device_id_type=LOGICAL,
        ).start()
        return carry

    def pack_all(quad, grid, first):
        def pack(i, carry):
            ty = 4 * i
            new = stepped(grid, STEPS - 1, first, first + PLANES, ty, 4)
            at_plane = [new[(x - first) % PLANES] for x in range(PLANES)]
            for h in range(2):
                tiles = []
                for x in range(4):
                    a, b = at_plane[x], at_plane[4 + x]
                    if h == 0:
                        tiles.append(jnp.where(upper_half, a, pltpu.roll(b, 4, 1)))
                    else:
                        tiles.append(jnp.where(upper_half, pltpu.roll(a, 4, 1), b))
                for j, tile in enumerate(swap_lanes(tiles, lane)):
                    for k in range(4):
                        at = 64 * h + 32 * (j // 2) + 2 * k + j % 2
                        outgoing[at + 2 * ty, quad] = tile[k]
            return carry

        lax.fori_loop(0, 4, pack, 0)

    halo_0.wait_send()
    halo_1b.start()
    halo_0.wait_recv()
    for level in range(STEPS - 1):
        advance(grids[0], level, 0, level + 3)
    pack_all(0, grids[0], 0)
    send_all(0)
    share_rates.wait_recv()
    take_rates(c_next, STEPS, PLANES)
    back_halo.wait_recv()
    wrap(ahead, 0, PLANES, PLANES + STEPS)
    for level in range(STEPS - 1):
        advance(ahead, level, PLANES, PLANES + STEPS)
    pack_all(2, ahead, STEPS)
    send_all(2)
    halo_1a.wait_recv()
    for level in range(3):
        advance(grids[1], level, 0, level + 3)
    halo_1b.wait_recv()
    for level in range(3, STEPS - 1):
        advance(grids[1], level, 0, level + 3)
    pack_all(1, grids[1], 0)
    lax.fori_loop(1, DEVICES, send_last, 0, unroll=2)
    incoming[s * GROUPS + g] = outgoing[me]

    edge_copy(0).wait_recv()
    edge_copy(1).wait_recv()
    maps[BLOCKS] = edge_in[1]
    maps[BLOCKS + 1] = edge_in[0]
    acc[...] = jnp.zeros(acc.shape, jnp.float32)

    half_row = iota((12, 8, LANES), 1) < 4
    pad = jnp.zeros((LANES - MEMBERS, CELLS), jnp.bfloat16)

    late = (iota((GROUPS, 8, LANES), 1) >= 4) & (iota((GROUPS, 8, LANES), 2) >= 64)
    for quad in (0, 2):
        most = incoming.at[pl.ds(0, DEVICES - 1), quad]
        pltpu.make_async_copy(most, most, early_sem.at[quad]).wait()
    seven = incoming.at[pl.ds(0, GROUPS - 1), 1]
    pltpu.make_async_copy(seven, seven, recv_sem.at[s]).wait()

    def gather(i, carry):
        slabs = [slab_of(i >> 1, 2 * (i & 1) + k, -1) for k in range(2)]
        eight = incoming.at[pl.ds(0, GROUPS), 1]

        @pl.when(i > 0)
        def _():
            pltpu.make_async_copy(eight, eight, recv_sem.at[slabs[0]]).wait()

        pltpu.make_async_copy(eight, eight, recv_sem.at[slabs[1]]).wait()
        highs, lows, sides = [], [], []
        for k in range(2):
            from_slab = slabs[k]
            before = (from_slab - 1) & (SLABS - 1)
            got = incoming[pl.ds(GROUPS * from_slab, GROUPS)]
            third = jnp.where(late, got[:, 2], incoming[pl.ds(GROUPS * before, GROUPS), 2])
            got = jnp.concatenate([got[:, :2], third[:, None]], axis=1)
            got = got.reshape(4, 2, QUADS, 8, LANES)
            a = got[:, 0].reshape(12, 8, LANES)
            b = got[:, 1].reshape(12, 8, LANES)
            near = jnp.where(half_row, a, pltpu.roll(b, 4, 1)).reshape(MEMBERS, LANES)
            far = jnp.where(half_row, pltpu.roll(a, 4, 1), b).reshape(MEMBERS, LANES)
            field = jnp.concatenate([near, far], axis=1)
            mean = jnp.sum(field, axis=0, keepdims=True) * (1.0 / MEMBERS)
            mean_of[from_slab] = mean
            away = field - mean
            high, low = halves(away)
            right_side = jnp.concatenate([high, pad, low, pad], axis=0)
            split[from_slab] = right_side
            pieces = []
            for b in range(BLOCKS + 2):
                omega = maps[b, pl.ds(from_slab, 1)]
                v = maps[b, pl.ds(SLABS + from_slab, 1)]
                pieces.append(omega * away)
                pieces.append(jnp.broadcast_to(v - mean * omega, (ROWS - MEMBERS, CELLS)))
            lhs_high, lhs_low = halves(jnp.concatenate(pieces, axis=0))
            highs.append(lhs_high)
            lows.append(lhs_low)
            sides.append(right_side)
        side = jnp.concatenate(sides, axis=1)
        high_part = nt(jnp.concatenate(highs, axis=1), side)
        low_part = nt(jnp.concatenate(lows, axis=1), side[:LANES])
        total = high_part[:, :LANES] + high_part[:, LANES:] + low_part
        acc[...] += total.reshape(acc.shape)
        return carry

    lax.fori_loop(0, SLABS // 2, gather, 0)

    def part_copy(side):
        return pltpu.make_async_remote_copy(
            src_ref=acc.at[BLOCKS + side],
            dst_ref=part_in.at[side],
            send_sem=part_send.at[side],
            recv_sem=part_recv.at[side],
            device_id=(left, right)[side],
            device_id_type=LOGICAL,
        )

    part_copy(0).start()
    part_copy(1).start()

    identity = jnp.where((spot == across) & (spot < MEMBERS), one, zero)[:MEMBERS]
    part_copy(0).wait_recv()
    part_copy(1).wait_recv()
    totals = [acc[b] for b in range(BLOCKS)]
    totals[BLOCKS - 1] = totals[BLOCKS - 1] + part_in[0]
    totals[0] = totals[0] + part_in[1]
    grams = [identity + t[:MEMBERS] for t in totals]
    fros = [jnp.sqrt(jnp.sum(t * t, keepdims=True)) for t in grams]
    a_of = [t / f for t, f in zip(grams, fros)]
    middles = [1.5 * identity - 0.5 * a for a in a_of]
    z_of = middles
    a_of = [product(a, r) for a, r in zip(a_of, middles)]
    for iteration in range(1, ITERS):
        middles = [1.5 * identity - 0.5 * product(z, a) for z, a in zip(z_of, a_of)]
        if iteration < ITERS - 1:
            a_of = [product(a, r) for a, r in zip(a_of, middles)]
        z_of = [product(r, z) for r, z in zip(middles, z_of)]
    for b in range(BLOCKS):
        transform = z_of[b] * (1.0 / jnp.sqrt(fros[b]))
        projected = jnp.broadcast_to(totals[b][MEMBERS : MEMBERS + 1], (16, LANES))
        mean_weights = product(product(projected, transform), transform)[:1]
        high, low = halves(transform)
        both = nn(select[...], jnp.concatenate([padded(high), padded(low)], axis=1))
        by_member = (both[:MEMBERS, :LANES] + both[:MEMBERS, LANES:]) + mean_weights
        high, low = halves(by_member)
        ordered[0, MEMBERS * b : MEMBERS * (b + 1)] = jnp.concatenate([high, high], axis=1)
        ordered[1, MEMBERS * b : MEMBERS * (b + 1)] = jnp.concatenate([low, low], axis=1)

    for quad in range(QUADS):
        most = outgoing.at[pl.ds(0, DEVICES - 1), quad]
        pltpu.make_async_copy(most, most, send_sem.at[quad]).wait()

    block_of = (iota((MEMBERS, CELLS), 1) % OWN) // TILE_WIDTH

    def give_back(i, carry):
        to_slabs = []
        for c in range(4):
            to_slab = slab_of(i, c, 1)
            to_slabs.append(to_slab)
            right_side = split[to_slab]
            parts = nn(ordered[0], right_side) + nn(ordered[1], right_side)
            field = parts[:MEMBERS]
            for b in range(1, BLOCKS):
                field = jnp.where(block_of == b, parts[MEMBERS * b : MEMBERS * (b + 1)], field)
            field = field + mean_of[to_slab]
            near = field[:, :LANES].reshape(12, 8, LANES)
            far = field[:, LANES:].reshape(12, 8, LANES)
            even = jnp.where(half_row, near, pltpu.roll(far, 4, 1)).reshape(4, QUADS, 8, LANES)
            odd = jnp.where(half_row, pltpu.roll(near, 4, 1), far).reshape(4, QUADS, 8, LANES)
            for a in range(4):
                incoming[GROUPS * to_slab + 2 * a] = even[a]
                incoming[GROUPS * to_slab + 2 * a + 1] = odd[a]

        def to_group(j, carry):
            for c in range(4):
                peer_g = (g + j + 2 * c) & (GROUPS - 1)

                def start():
                    pltpu.make_async_remote_copy(
                        src_ref=incoming.at[GROUPS * to_slabs[c] + peer_g],
                        dst_ref=returned.at[me],
                        send_sem=back_send,
                        recv_sem=back_recv,
                        device_id=peer_g * SLABS + to_slabs[c],
                        device_id_type=LOGICAL,
                    ).start()

                if c == 0:
                    pl.when(i * GROUPS + j > 0)(start)
                else:
                    start()
            return carry

        lax.fori_loop(0, GROUPS, to_group, 0)
        return carry

    lax.fori_loop(0, 4, give_back, 0)
    returned[me] = incoming[s * GROUPS + g]

    for copy in (halo_1a, halo_1b, back_halo, back_rates, share_rates):
        copy.wait_send()
    for side in range(2):
        edge_copy(side).wait_send()
        part_copy(side).wait_send()
    sent = incoming.at[pl.ds(0, DEVICES - 1)]
    pltpu.make_async_copy(sent, sent, back_send).wait()
    got = returned.at[pl.ds(0, DEVICES - 1)]
    pltpu.make_async_copy(got, got, back_recv).wait()

    def unpack(tile, carry):
        for quad in range(QUADS):
            tiles = swap_lanes([returned[4 * tile + q, quad] for q in range(4)], lane)
            tiles = swap_rows(tiles, row)
            for i in range(4):
                o_ref[4 * quad + i, tile] = tiles[i]
        return carry

    lax.fori_loop(0, TILES, unpack, 0, unroll=4)


def shards(
    initial_samples,
    transport_ratios,
    assignment,
    obs_values,
    obs_error,
    sensor_easting_offset,
    obs_column,
    obs_count,
):
    members, planes, columns = initial_samples.shape

    def tiled(x):
        return jnp.transpose(x.reshape(-1, planes, TILES, LANES), (0, 2, 1, 3))

    f32 = jnp.float32
    i32 = jnp.int32
    bf16 = jnp.bfloat16
    dma = pltpu.SemaphoreType.DMA
    hbm = pl.BlockSpec(memory_space=pltpu.HBM)
    out = pl.pallas_call(
        kernel,
        name="analysis",
        out_shape=jax.ShapeDtypeStruct((members, TILES, planes, LANES), f32),
        in_specs=[hbm] * 8,
        out_specs=pl.BlockSpec(memory_space=pltpu.VMEM),
        scratch_shapes=[
            pltpu.VMEM((4 * QUADS, TILES, PLANES, LANES), f32),
            pltpu.VMEM((3, TILES, PLANES, LANES), f32),
            pltpu.VMEM((1, MEMBERS), i32),
            pltpu.VMEM((BLOCKS, OBS), f32),
            pltpu.VMEM((BLOCKS, OBS), f32),
            pltpu.VMEM((BLOCKS, OBS), i32),
            pltpu.VMEM((BLOCKS, OBS), i32),
            pltpu.VMEM((1, BLOCKS), i32),
            pltpu.VMEM((3, TILES, PLANES, LANES), f32),
            pltpu.VMEM((3, PLANES + STEPS, 16, 8, LANES), f32),
            pltpu.VMEM((2, STEPS, PLANES + 1, 17, 8, LANES), f32),
            pltpu.VMEM((STEPS, PLANES + STEPS + 1, 17, 8, LANES), f32),
            pltpu.VMEM((DEVICES, QUADS, 8, LANES), f32),
            pltpu.VMEM((DEVICES, QUADS, 8, LANES), f32),
            pltpu.VMEM((DEVICES, QUADS, 8, LANES), f32),
            pltpu.VMEM((SLABS, 2 * LANES, CELLS), bf16),
            pltpu.VMEM((SLABS, 1, CELLS), f32),
            pltpu.VMEM((BLOCKS + 2, 2 * SLABS, CELLS), f32),
            pltpu.VMEM((2, 2 * SLABS, CELLS), f32),
            pltpu.VMEM((2, 2 * SLABS, CELLS), f32),
            pltpu.VMEM((BLOCKS + 2, ROWS, LANES), f32),
            pltpu.VMEM((2, ROWS, LANES), f32),
            pltpu.VMEM((LANES, LANES), bf16),
            pltpu.VMEM((2, BLOCKS * MEMBERS, 2 * LANES), bf16),
            dma((QUADS,)),
            dma((7,)),
            dma((6,)),
            dma((6,)),
            dma((2,)),
            dma((2,)),
            dma((2,)),
            dma((2,)),
            dma((QUADS,)),
            dma((QUADS,)),
            dma((SLABS,)),
            dma,
            dma,
            pltpu.SemaphoreType.REGULAR,
        ],
        compiler_params=pltpu.CompilerParams(
            collective_id=0, has_side_effects=True, vmem_limit_bytes=56 << 20
        ),
    )(
        tiled(initial_samples),
        tiled(transport_ratios),
        assignment[None, :],
        obs_values,
        obs_error,
        sensor_easting_offset,
        obs_column,
        obs_count[None, :],
    )
    return jnp.transpose(out, (0, 2, 1, 3)).reshape(members, planes, columns)


def solution(mesh):
    placed = (
        P("group", "slab", None),
        P(None, "slab", None),
        P(),
        P(("group", "slab"), None),
        P(("group", "slab"), None),
        P(("group", "slab"), None),
        P(("group", "slab"), None),
        P(("group", "slab")),
    )
    return jax.shard_map(
        shards, mesh=mesh, in_specs=placed, out_specs=P("group", "slab", None), check_vma=False
    )
```

```python
import jax
import jax.numpy as jnp
from jax import lax
from jax.experimental import pallas as pl
from jax.experimental.pallas import tpu as pltpu
from jax.sharding import PartitionSpec as P

MEMBERS = 96
NZ = 64
STEPS = 6
TILE_WIDTH = 8
HC = 8
OBS = 512
ITERS = 8

GROUPS = 8
SLABS = 16
DEVICES = GROUPS * SLABS
PLANES = 8
TILES = 32
LANES = 128
QUADS = 3
OWN = 32
BLOCKS = 4
CELLS = PLANES * OWN
ROWS = 112
LOGICAL = pl.DeviceIdType.LOGICAL


def nt(a, b):
    return lax.dot_general(a, b, (((1,), (1,)), ((), ())), preferred_element_type=jnp.float32)


def nn(a, b):
    return lax.dot_general(a, b, (((1,), (0,)), ((), ())), preferred_element_type=jnp.float32)


def halves(a):
    high = a.astype(jnp.bfloat16)
    return high, (a - high.astype(jnp.float32)).astype(jnp.bfloat16)


def padded(a):
    return jnp.concatenate([a, jnp.zeros((LANES - MEMBERS, LANES), a.dtype)], axis=0)


def product(a, b):
    ah, al = halves(a)
    bh, bl = halves(b)
    bh, bl = padded(bh), padded(bl)
    top = jnp.concatenate([bh, bl], axis=1)
    bottom = jnp.concatenate([bh, jnp.zeros_like(bl)], axis=1)
    both = nn(jnp.concatenate([ah, al], axis=1), jnp.concatenate([top, bottom], axis=0))
    return both[:, :LANES] + both[:, LANES:]


def swap_rows(tiles, row):
    axis = tiles[0].ndim - 2
    t0, t1, t2, t3 = tiles
    up = (row & 2) == 0
    b0 = jnp.where(up, t0, pltpu.roll(t2, 2, axis))
    b2 = jnp.where(up, pltpu.roll(t0, 6, axis), t2)
    b1 = jnp.where(up, t1, pltpu.roll(t3, 2, axis))
    b3 = jnp.where(up, pltpu.roll(t1, 6, axis), t3)
    even = (row & 1) == 0
    o0 = jnp.where(even, b0, pltpu.roll(b1, 1, axis))
    o1 = jnp.where(even, pltpu.roll(b0, 7, axis), b1)
    o2 = jnp.where(even, b2, pltpu.roll(b3, 1, axis))
    o3 = jnp.where(even, pltpu.roll(b2, 7, axis), b3)
    return o0, o1, o2, o3


def swap_lanes(tiles, lane):
    axis = tiles[0].ndim - 1
    t0, t1, t2, t3 = tiles
    low = (lane & 64) == 0
    b0 = jnp.where(low, t0, pltpu.roll(t2, 64, axis))
    b2 = jnp.where(low, pltpu.roll(t0, 64, axis), t2)
    b1 = jnp.where(low, t1, pltpu.roll(t3, 64, axis))
    b3 = jnp.where(low, pltpu.roll(t1, 64, axis), t3)
    even = (lane & 32) == 0
    o0 = jnp.where(even, b0, pltpu.roll(b1, 32, axis))
    o1 = jnp.where(even, pltpu.roll(b0, 96, axis), b1)
    o2 = jnp.where(even, b2, pltpu.roll(b3, 32, axis))
    o3 = jnp.where(even, pltpu.roll(b2, 96, axis), b3)
    return o0, o1, o2, o3


def iota(shape, dim):
    return lax.broadcasted_iota(jnp.int32, shape, dim)


def transposed(tiles, row):
    axis = tiles[0].ndim - 2
    tiles = list(tiles)
    for d in (4, 2, 1):
        upper = (row & d) == 0
        for j in range(8):
            if not j & d:
                a, b = tiles[j], tiles[j + d]
                tiles[j] = jnp.where(upper, a, pltpu.roll(b, d, axis))
                tiles[j + d] = jnp.where(upper, pltpu.roll(a, 8 - d, axis), b)
    return tiles


def kernel(
    x_hbm,
    c_hbm,
    asg_hbm,
    val_hbm,
    err_hbm,
    east_hbm,
    col_hbm,
    cnt_hbm,
    o_ref,
    x_ref,
    c_ref,
    asg_ref,
    val_ref,
    err_ref,
    east_ref,
    col_ref,
    cnt_ref,
    c_next,
    rates,
    state,
    ahead,
    outgoing,
    incoming,
    returned,
    split,
    mean_of,
    maps,
    edge_out,
    edge_in,
    acc,
    part_in,
    select,
    ordered,
    x_sem,
    small_sem,
    halo_send,
    halo_recv,
    edge_send,
    edge_recv,
    part_send,
    part_recv,
    send_sem,
    early_sem,
    recv_sem,
    back_send,
    back_recv,
    everyone,
):
    g = lax.axis_index("group")
    s = lax.axis_index("slab")
    me = g * SLABS + s
    left = (me + DEVICES - 1) % DEVICES
    right = (me + 1) % DEVICES

    rate_copy = pltpu.make_async_copy(c_hbm, c_ref, small_sem.at[0])
    rate_copy.start()

    def sample_copy(quad):
        four = pl.ds(4 * quad, 4)
        return pltpu.make_async_copy(x_hbm.at[four], x_ref.at[four], x_sem.at[quad])

    for quad in range(QUADS):
        sample_copy(quad).start()
    small_copies = [
        pltpu.make_async_copy(source, target, small_sem.at[1 + i])
        for i, (source, target) in enumerate(
            [
                (asg_hbm, asg_ref),
                (val_hbm, val_ref),
                (err_hbm, err_ref),
                (east_hbm, east_ref),
                (col_hbm, col_ref),
                (cnt_hbm, cnt_ref),
            ]
        )
    ]
    for copy in small_copies:
        copy.start()

    barrier = pltpu.get_barrier_semaphore()

    def group_peer(i):
        return ((g + i) & (GROUPS - 1)) * SLABS + s

    def slab_peer(i):
        return g * SLABS + ((s + i) & (SLABS - 1))

    for i in range(1, SLABS):
        pl.semaphore_signal(
            barrier, inc=1, device_id=slab_peer(i), device_id_type=LOGICAL
        )
    for i in range(1, GROUPS):
        pl.semaphore_signal(
            barrier, inc=1, device_id=group_peer(i), device_id_type=LOGICAL
        )

    row = iota((8, LANES), 0)
    lane = iota((8, LANES), 1)
    upper_half = row < 4
    low_half = lane < 64
    z_first = (lane & (NZ - 1)) == 0

    def lanes_swapped(a, b):
        first = jnp.where(low_half, a, pltpu.roll(b, 64, 1))
        second = jnp.where(low_half, pltpu.roll(a, 64, 1), b)
        return jnp.stack([first, second])

    rate_copy.wait()

    def take_rates(source, planes, offset):
        def one(u, carry):
            for i in range(3):
                sides = [
                    lanes_swapped(source[i, u + 16 * h], source[i, u + 16 * h + 8])
                    for h in range(2)
                ]
                for x in range(planes):
                    rates[i, offset + x, pl.ds(2 * u, 2)] = jnp.where(
                        upper_half, sides[0][:, x : x + 1], sides[1][:, x : x + 1]
                    )
            return carry

        lax.fori_loop(0, 8, one, 0)

    take_rates(c_ref, PLANES, 0)

    def wrap(grid, level, first, end):
        last = grid[level, first + 1 : end + 1, 16]
        turned = pltpu.roll(last, 64, 2)
        grid[level, first + 1 : end + 1, 0] = jnp.where(
            low_half, pltpu.roll(turned, 4, 1), turned
        )

    def take_samples(quad, grid):
        sample_copy(quad).wait()

        def one(u, carry):
            tiles = []
            for h in range(2):
                for i in range(4):
                    at = 4 * quad + i
                    tiles.append(lanes_swapped(x_ref[at, u + 16 * h], x_ref[at, u + 16 * h + 8]))
            for x, tile in enumerate(transposed(tiles, row)):
                grid[0, x + 1, pl.ds(2 * u + 1, 2)] = tile
            return carry

        lax.fori_loop(0, 8, one, 0)
        wrap(grid, 0, 0, PLANES)

    def stepped(grid, level, first, end, ty, n):
        u = grid[level, first + 1 : end + 1, pl.ds(ty + 1, n)]
        above = grid[level, first:end, pl.ds(ty + 1, n)]
        below_y = grid[level, first + 1 : end + 1, pl.ds(ty, n)]
        below_z = jnp.where(z_first, pltpu.roll(u, 65, 3), pltpu.roll(u, 1, 3))
        return (
            u
            - rates[0, first:end, pl.ds(ty, n)] * (u - above)
            - rates[1, first:end, pl.ds(ty, n)] * (u - below_y)
            - rates[2, first:end, pl.ds(ty, n)] * (u - below_z)
        )

    def advance(grid, level, first, end):
        planes = end - first
        n = 16 if planes < 4 else 8

        def one(i, carry):
            new = stepped(grid, level, first, end, n * i, n)
            grid[level + 1, first + 1 : end + 1, pl.ds(n * i + 1, n)] = new
            return carry

        lax.fori_loop(0, 16 // n, one, 0)
        wrap(grid, level + 1, first, end)

    next_slab = g * SLABS + ((s + 1) & (SLABS - 1))
    last_slab = g * SLABS + ((s + SLABS - 1) & (SLABS - 1))

    def halo_copy(quad, low, high, sem):
        levels = pl.ds(low, high - low)
        return pltpu.make_async_remote_copy(
            src_ref=state.at[quad, levels, PLANES, pl.ds(1, 16)],
            dst_ref=state.at[quad, levels, 0, pl.ds(1, 16)],
            send_sem=halo_send.at[sem],
            recv_sem=halo_recv.at[sem],
            device_id=next_slab,
            device_id_type=LOGICAL,
        )

    halo_0a = halo_copy(0, 0, 3, 0)
    halo_0b = halo_copy(0, 3, STEPS, 6)
    halo_1a = halo_copy(1, 0, 3, 1)
    halo_1b = halo_copy(1, 3, STEPS, 2)

    back_halo = pltpu.make_async_remote_copy(
        src_ref=ahead.at[0, pl.ds(1, STEPS), pl.ds(1, 16)],
        dst_ref=ahead.at[0, pl.ds(PLANES + 1, STEPS), pl.ds(1, 16)],
        send_sem=halo_send.at[3],
        recv_sem=halo_recv.at[3],
        device_id=last_slab,
        device_id_type=LOGICAL,
    )
    half = pl.ds((g & 1) * (TILES // 2), TILES // 2)
    back_rates = pltpu.make_async_remote_copy(
        src_ref=c_ref.at[:, half],
        dst_ref=c_next.at[:, half],
        send_sem=halo_send.at[4],
        recv_sem=halo_recv.at[4],
        device_id=last_slab,
        device_id_type=LOGICAL,
    )
    share_rates = pltpu.make_async_remote_copy(
        src_ref=c_next.at[:, half],
        dst_ref=c_next.at[:, half],
        send_sem=halo_send.at[5],
        recv_sem=halo_recv.at[5],
        device_id=(g ^ 1) * SLABS + s,
        device_id_type=LOGICAL,
    )

    grids = [state.at[0], state.at[1]]

    def own_cone(quad):
        take_samples(quad, grids[quad])
        for level in range(STEPS - 1):
            advance(grids[quad], level, level + 3, PLANES)

    take_samples(0, grids[0])
    for level in range(2):
        advance(grids[0], level, level + 3, PLANES)
    pl.semaphore_wait(barrier, SLABS + GROUPS - 2)
    halo_0a.start()
    back_rates.start()
    for level in range(2, STEPS - 1):
        advance(grids[0], level, level + 3, PLANES)
    halo_0b.start()
    for i in range(1, GROUPS):
        pl.semaphore_signal(everyone, inc=1, device_id=group_peer(i), device_id_type=LOGICAL)
    take_samples(2, ahead)
    back_halo.start()
    own_cone(1)
    halo_1a.start()
    for level in range(STEPS - 1):
        advance(ahead, level, level + 1, PLANES)
    back_rates.wait_recv()
    share_rates.start()

    for copy in small_copies:
        copy.wait()

    slots = iota((1, OBS), 1)
    for b in range(BLOCKS):
        live = slots < cnt_ref[:, b : b + 1]
        square = jnp.where(live, 1.0 / (err_ref[b : b + 1, :] * (MEMBERS - 1.0)), 0.0)
        valued = square * val_ref[b : b + 1, :]
        easting = east_ref[b : b + 1, :]
        column = TILE_WIDTH * b - HC + col_ref[b : b + 1, :]
        at_slab = iota((SLABS, OBS), 0) == (easting >> 3)
        left_side = jnp.concatenate(
            [jnp.where(at_slab, square, 0.0), jnp.where(at_slab, valued, 0.0)], axis=0
        )
        high, low = halves(left_side)
        both = jnp.concatenate([high, low], axis=0)
        cell = iota((CELLS, OBS), 0)
        base = (easting & (PLANES - 1)) * OWN

        def spread(inside, offset):
            at = jnp.where(inside, base + column + offset, -1)
            hot = jnp.where(cell == at, 1.0, 0.0).astype(jnp.bfloat16)
            got = nt(both, hot)
            return got[: 2 * SLABS] + got[2 * SLABS :]

        maps[b] = spread((column >= 0) & (column < OWN), 0)
        if b == 0:
            edge_out[0] = spread(column < 0, OWN)
        if b == BLOCKS - 1:
            edge_out[1] = spread(column >= OWN, -OWN)

    def edge_copy(side):
        return pltpu.make_async_remote_copy(
            src_ref=edge_out.at[side],
            dst_ref=edge_in.at[side],
            send_sem=edge_send.at[side],
            recv_sem=edge_recv.at[side],
            device_id=(left, right)[side],
            device_id_type=LOGICAL,
        )

    pl.semaphore_wait(everyone, GROUPS - 1)
    edge_copy(0).start()
    edge_copy(1).start()

    spot = iota((LANES, LANES), 0)
    across = iota((LANES, LANES), 1)

    def member(r):
        return 24 * (r // 24) + 12 * ((r // 4) % 2) + 4 * ((r // 8) % 3) + r % 4

    one = jnp.float32(1.0)
    zero = jnp.float32(0.0)
    slot_lane = iota((LANES, MEMBERS), 1)
    slot_spot = iota((LANES, MEMBERS), 0)
    hot = jnp.where(asg_ref[...] == slot_spot, one, zero).astype(jnp.bfloat16)
    order = jnp.where((member(spot) == across) & (spot < MEMBERS), one, zero).astype(jnp.bfloat16)
    slot_order = jnp.where((member(slot_spot) == slot_lane) & (slot_spot < MEMBERS), one, zero)
    member_rows = nn(order, hot).astype(jnp.bfloat16)
    select[...] = nt(member_rows, slot_order.astype(jnp.bfloat16)).astype(jnp.bfloat16)

    def send_all(quad):
        def send(k, carry):
            peer = (((g + (k >> 4)) & (GROUPS - 1)) * SLABS) + ((s + k) & (SLABS - 1))
            pltpu.make_async_remote_copy(
                src_ref=outgoing.at[peer, quad],
                dst_ref=incoming.at[s * GROUPS + g, quad],
                send_sem=send_sem.at[quad],
                recv_sem=early_sem.at[quad],
                device_id=peer,
                device_id_type=LOGICAL,
            ).start()
            return carry

        lax.fori_loop(1, DEVICES, send, 0, unroll=2)

    def slab_of(i, c, sign):
        z = (s >> 2) + sign * (c + i)
        y = s + sign * c
        return ((z & 3) << 2) | (y & 3)

    def send_last(k, carry):
        peer_g = (g + (k >> 2) + 2 * k) & (GROUPS - 1)
        peer_s = slab_of(k >> 5, k & 3, 1)
        peer = peer_g * SLABS + peer_s
        pltpu.make_async_remote_copy(
            src_ref=outgoing.at[peer, 1],
            dst_ref=incoming.at[s * GROUPS + g, 1],
            send_sem=send_sem.at[1],
            recv_sem=recv_sem.at[s],
            device_id=peer,
            device_id_type=LOGICAL,
        ).start()
        return carry

    def pack_all(quad, grid, first):
        def pack(i, carry):
            ty = 4 * i
            new = stepped(grid, STEPS - 1, first, first + PLANES, ty, 4)
            at_plane = [new[(x - first) % PLANES] for x in range(PLANES)]
            for h in range(2):
                tiles = []
                for x in range(4):
                    a, b = at_plane[x], at_plane[4 + x]
                    if h == 0:
                        tiles.append(jnp.where(upper_half, a, pltpu.roll(b, 4, 1)))
                    else:
                        tiles.append(jnp.where(upper_half, pltpu.roll(a, 4, 1), b))
                for j, tile in enumerate(swap_lanes(tiles, lane)):
                    for k in range(4):
                        at = 64 * h + 32 * (j // 2) + 2 * k + j % 2
                        outgoing[at + 2 * ty, quad] = tile[k]
            return carry

        lax.fori_loop(0, 4, pack, 0)

    halo_0b.wait_send()
    halo_1b.start()
    halo_0a.wait_recv()
    for level in range(3):
        advance(grids[0], level, 0, level + 3)
    halo_0b.wait_recv()
    for level in range(3, STEPS - 1):
        advance(grids[0], level, 0, level + 3)
    pack_all(0, grids[0], 0)
    share_rates.wait_recv()
    take_rates(c_next, STEPS, PLANES)
    back_halo.wait_recv()
    wrap(ahead, 0, PLANES, PLANES + STEPS)
    for level in range(STEPS - 1):
        advance(ahead, level, PLANES, PLANES + STEPS)
    pack_all(2, ahead, STEPS)
    send_all(0)
    send_all(2)
    halo_1a.wait_recv()
    for level in range(3):
        advance(grids[1], level, 0, level + 3)
    halo_1b.wait_recv()
    for level in range(3, STEPS - 1):
        advance(grids[1], level, 0, level + 3)
    pack_all(1, grids[1], 0)
    lax.fori_loop(1, DEVICES, send_last, 0, unroll=2)
    incoming[s * GROUPS + g] = outgoing[me]

    edge_copy(0).wait_recv()
    edge_copy(1).wait_recv()
    maps[BLOCKS] = edge_in[1]
    maps[BLOCKS + 1] = edge_in[0]
    acc[...] = jnp.zeros(acc.shape, jnp.float32)

    half_row = iota((12, 8, LANES), 1) < 4
    pad = jnp.zeros((LANES - MEMBERS, CELLS), jnp.bfloat16)

    late = (iota((GROUPS, 8, LANES), 1) >= 4) & (iota((GROUPS, 8, LANES), 2) >= 64)
    for quad in (0, 2):
        most = incoming.at[pl.ds(0, DEVICES - 1), quad]
        pltpu.make_async_copy(most, most, early_sem.at[quad]).wait()
    seven = incoming.at[pl.ds(0, GROUPS - 1), 1]
    pltpu.make_async_copy(seven, seven, recv_sem.at[s]).wait()

    def gather(i, carry):
        slabs = [slab_of(i >> 1, 2 * (i & 1) + k, -1) for k in range(2)]
        eight = incoming.at[pl.ds(0, GROUPS), 1]

        @pl.when(i > 0)
        def _():
            pltpu.make_async_copy(eight, eight, recv_sem.at[slabs[0]]).wait()

        pltpu.make_async_copy(eight, eight, recv_sem.at[slabs[1]]).wait()
        highs, lows, sides = [], [], []
        for k in range(2):
            from_slab = slabs[k]
            before = (from_slab - 1) & (SLABS - 1)
            got = incoming[pl.ds(GROUPS * from_slab, GROUPS)]
            third = jnp.where(late, got[:, 2], incoming[pl.ds(GROUPS * before, GROUPS), 2])
            got = jnp.concatenate([got[:, :2], third[:, None]], axis=1)
            got = got.reshape(4, 2, QUADS, 8, LANES)
            a = got[:, 0].reshape(12, 8, LANES)
            b = got[:, 1].reshape(12, 8, LANES)
            near = jnp.where(half_row, a, pltpu.roll(b, 4, 1)).reshape(MEMBERS, LANES)
            far = jnp.where(half_row, pltpu.roll(a, 4, 1), b).reshape(MEMBERS, LANES)
            field = jnp.concatenate([near, far], axis=1)
            mean = jnp.sum(field, axis=0, keepdims=True) * (1.0 / MEMBERS)
            mean_of[from_slab] = mean
            away = field - mean
            high, low = halves(away)
            right_side = jnp.concatenate([high, pad, low, pad], axis=0)
            split[from_slab] = right_side
            pieces = []
            for b in range(BLOCKS + 2):
                omega = maps[b, pl.ds(from_slab, 1)]
                v = maps[b, pl.ds(SLABS + from_slab, 1)]
                pieces.append(omega * away)
                pieces.append(jnp.broadcast_to(v - mean * omega, (ROWS - MEMBERS, CELLS)))
            lhs_high, lhs_low = halves(jnp.concatenate(pieces, axis=0))
            highs.append(lhs_high)
            lows.append(lhs_low)
            sides.append(right_side)
        side = jnp.concatenate(sides, axis=1)
        high_part = nt(jnp.concatenate(highs, axis=1), side)
        low_part = nt(jnp.concatenate(lows, axis=1), side[:LANES])
        total = high_part[:, :LANES] + high_part[:, LANES:] + low_part
        acc[...] += total.reshape(acc.shape)
        return carry

    lax.fori_loop(0, SLABS // 2, gather, 0)

    def part_copy(side):
        return pltpu.make_async_remote_copy(
            src_ref=acc.at[BLOCKS + side],
            dst_ref=part_in.at[side],
            send_sem=part_send.at[side],
            recv_sem=part_recv.at[side],
            device_id=(left, right)[side],
            device_id_type=LOGICAL,
        )

    part_copy(0).start()
    part_copy(1).start()

    identity = jnp.where((spot == across) & (spot < MEMBERS), one, zero)[:MEMBERS]
    part_copy(0).wait_recv()
    part_copy(1).wait_recv()
    totals = [acc[b] for b in range(BLOCKS)]
    totals[BLOCKS - 1] = totals[BLOCKS - 1] + part_in[0]
    totals[0] = totals[0] + part_in[1]
    grams = [identity + t[:MEMBERS] for t in totals]
    fros = [jnp.sqrt(jnp.sum(t * t, keepdims=True)) for t in grams]
    a_of = [t / f for t, f in zip(grams, fros)]
    middles = [1.5 * identity - 0.5 * a for a in a_of]
    z_of = middles
    a_of = [product(a, r) for a, r in zip(a_of, middles)]
    for iteration in range(1, ITERS):
        middles = [1.5 * identity - 0.5 * product(z, a) for z, a in zip(z_of, a_of)]
        if iteration < ITERS - 1:
            a_of = [product(a, r) for a, r in zip(a_of, middles)]
        z_of = [product(r, z) for r, z in zip(middles, z_of)]
    for b in range(BLOCKS):
        transform = z_of[b] * (1.0 / jnp.sqrt(fros[b]))
        projected = jnp.broadcast_to(totals[b][MEMBERS : MEMBERS + 1], (16, LANES))
        mean_weights = product(product(projected, transform), transform)[:1]
        high, low = halves(transform)
        both = nn(select[...], jnp.concatenate([padded(high), padded(low)], axis=1))
        by_member = (both[:MEMBERS, :LANES] + both[:MEMBERS, LANES:]) + mean_weights
        high, low = halves(by_member)
        ordered[0, MEMBERS * b : MEMBERS * (b + 1)] = jnp.concatenate([high, high], axis=1)
        ordered[1, MEMBERS * b : MEMBERS * (b + 1)] = jnp.concatenate([low, low], axis=1)

    for quad in range(QUADS):
        most = outgoing.at[pl.ds(0, DEVICES - 1), quad]
        pltpu.make_async_copy(most, most, send_sem.at[quad]).wait()

    block_of = (iota((MEMBERS, CELLS), 1) % OWN) // TILE_WIDTH

    def give_back(i, carry):
        to_slabs = []
        for c in range(4):
            to_slab = slab_of(i, c, 1)
            to_slabs.append(to_slab)
            right_side = split[to_slab]
            parts = nn(ordered[0], right_side) + nn(ordered[1], right_side)
            field = parts[:MEMBERS]
            for b in range(1, BLOCKS):
                field = jnp.where(block_of == b, parts[MEMBERS * b : MEMBERS * (b + 1)], field)
            field = field + mean_of[to_slab]
            near = field[:, :LANES].reshape(12, 8, LANES)
            far = field[:, LANES:].reshape(12, 8, LANES)
            even = jnp.where(half_row, near, pltpu.roll(far, 4, 1)).reshape(4, QUADS, 8, LANES)
            odd = jnp.where(half_row, pltpu.roll(near, 4, 1), far).reshape(4, QUADS, 8, LANES)
            for a in range(4):
                incoming[GROUPS * to_slab + 2 * a] = even[a]
                incoming[GROUPS * to_slab + 2 * a + 1] = odd[a]

        def to_group(j, carry):
            for c in range(4):
                peer_g = (g + j + 2 * c) & (GROUPS - 1)

                def start():
                    pltpu.make_async_remote_copy(
                        src_ref=incoming.at[GROUPS * to_slabs[c] + peer_g],
                        dst_ref=returned.at[me],
                        send_sem=back_send,
                        recv_sem=back_recv,
                        device_id=peer_g * SLABS + to_slabs[c],
                        device_id_type=LOGICAL,
                    ).start()

                if c == 0:
                    pl.when(i * GROUPS + j > 0)(start)
                else:
                    start()
            return carry

        lax.fori_loop(0, GROUPS, to_group, 0)
        return carry

    lax.fori_loop(0, 4, give_back, 0)
    returned[me] = incoming[s * GROUPS + g]

    for copy in (halo_0a, halo_1a, halo_1b, back_halo, back_rates, share_rates):
        copy.wait_send()
    for side in range(2):
        edge_copy(side).wait_send()
        part_copy(side).wait_send()
    sent = incoming.at[pl.ds(0, DEVICES - 1)]
    pltpu.make_async_copy(sent, sent, back_send).wait()
    got = returned.at[pl.ds(0, DEVICES - 1)]
    pltpu.make_async_copy(got, got, back_recv).wait()

    def unpack(tile, carry):
        for quad in range(QUADS):
            tiles = swap_lanes([returned[4 * tile + q, quad] for q in range(4)], lane)
            tiles = swap_rows(tiles, row)
            for i in range(4):
                o_ref[4 * quad + i, tile] = tiles[i]
        return carry

    lax.fori_loop(0, TILES, unpack, 0, unroll=4)


def shards(
    initial_samples,
    transport_ratios,
    assignment,
    obs_values,
    obs_error,
    sensor_easting_offset,
    obs_column,
    obs_count,
):
    members, planes, columns = initial_samples.shape

    def tiled(x):
        return jnp.transpose(x.reshape(-1, planes, TILES, LANES), (0, 2, 1, 3))

    f32 = jnp.float32
    i32 = jnp.int32
    bf16 = jnp.bfloat16
    dma = pltpu.SemaphoreType.DMA
    hbm = pl.BlockSpec(memory_space=pltpu.HBM)
    out = pl.pallas_call(
        kernel,
        name="analysis",
        out_shape=jax.ShapeDtypeStruct((members, TILES, planes, LANES), f32),
        in_specs=[hbm] * 8,
        out_specs=pl.BlockSpec(memory_space=pltpu.VMEM),
        scratch_shapes=[
            pltpu.VMEM((4 * QUADS, TILES, PLANES, LANES), f32),
            pltpu.VMEM((3, TILES, PLANES, LANES), f32),
            pltpu.VMEM((1, MEMBERS), i32),
            pltpu.VMEM((BLOCKS, OBS), f32),
            pltpu.VMEM((BLOCKS, OBS), f32),
            pltpu.VMEM((BLOCKS, OBS), i32),
            pltpu.VMEM((BLOCKS, OBS), i32),
            pltpu.VMEM((1, BLOCKS), i32),
            pltpu.VMEM((3, TILES, PLANES, LANES), f32),
            pltpu.VMEM((3, PLANES + STEPS, 16, 8, LANES), f32),
            pltpu.VMEM((2, STEPS, PLANES + 1, 17, 8, LANES), f32),
            pltpu.VMEM((STEPS, PLANES + STEPS + 1, 17, 8, LANES), f32),
            pltpu.VMEM((DEVICES, QUADS, 8, LANES), f32),
            pltpu.VMEM((DEVICES, QUADS, 8, LANES), f32),
            pltpu.VMEM((DEVICES, QUADS, 8, LANES), f32),
            pltpu.VMEM((SLABS, 2 * LANES, CELLS), bf16),
            pltpu.VMEM((SLABS, 1, CELLS), f32),
            pltpu.VMEM((BLOCKS + 2, 2 * SLABS, CELLS), f32),
            pltpu.VMEM((2, 2 * SLABS, CELLS), f32),
            pltpu.VMEM((2, 2 * SLABS, CELLS), f32),
            pltpu.VMEM((BLOCKS + 2, ROWS, LANES), f32),
            pltpu.VMEM((2, ROWS, LANES), f32),
            pltpu.VMEM((LANES, LANES), bf16),
            pltpu.VMEM((2, BLOCKS * MEMBERS, 2 * LANES), bf16),
            dma((QUADS,)),
            dma((7,)),
            dma((7,)),
            dma((7,)),
            dma((2,)),
            dma((2,)),
            dma((2,)),
            dma((2,)),
            dma((QUADS,)),
            dma((QUADS,)),
            dma((SLABS,)),
            dma,
            dma,
            pltpu.SemaphoreType.REGULAR,
        ],
        compiler_params=pltpu.CompilerParams(
            collective_id=0, has_side_effects=True, vmem_limit_bytes=56 << 20
        ),
    )(
        tiled(initial_samples),
        tiled(transport_ratios),
        assignment[None, :],
        obs_values,
        obs_error,
        sensor_easting_offset,
        obs_column,
        obs_count[None, :],
    )
    return jnp.transpose(out, (0, 2, 1, 3)).reshape(members, planes, columns)


def solution(mesh):
    placed = (
        P("group", "slab", None),
        P(None, "slab", None),
        P(),
        P(("group", "slab"), None),
        P(("group", "slab"), None),
        P(("group", "slab"), None),
        P(("group", "slab"), None),
        P(("group", "slab")),
    )
    return jax.shard_map(
        shards, mesh=mesh, in_specs=placed, out_specs=P("group", "slab", None), check_vma=False
    )
```

```python
import jax
import jax.numpy as jnp
from jax import lax
from jax.experimental import pallas as pl
from jax.experimental.pallas import tpu as pltpu
from jax.sharding import PartitionSpec as P

MEMBERS = 96
NZ = 64
STEPS = 6
TILE_WIDTH = 8
HC = 8
OBS = 512
ITERS = 8

GROUPS = 8
SLABS = 16
DEVICES = GROUPS * SLABS
PLANES = 8
TILES = 32
LANES = 128
QUADS = 3
OWN = 32
BLOCKS = 4
CELLS = PLANES * OWN
ROWS = 112
LOGICAL = pl.DeviceIdType.LOGICAL


def nt(a, b):
    return lax.dot_general(a, b, (((1,), (1,)), ((), ())), preferred_element_type=jnp.float32)


def nn(a, b):
    return lax.dot_general(a, b, (((1,), (0,)), ((), ())), preferred_element_type=jnp.float32)


def halves(a):
    high = a.astype(jnp.bfloat16)
    return high, (a - high.astype(jnp.float32)).astype(jnp.bfloat16)


def padded(a):
    return jnp.concatenate([a, jnp.zeros((LANES - MEMBERS, LANES), a.dtype)], axis=0)


def product(a, b):
    ah, al = halves(a)
    bh, bl = halves(b)
    bh, bl = padded(bh), padded(bl)
    top = jnp.concatenate([bh, bl], axis=1)
    bottom = jnp.concatenate([bh, jnp.zeros_like(bl)], axis=1)
    both = nn(jnp.concatenate([ah, al], axis=1), jnp.concatenate([top, bottom], axis=0))
    return both[:, :LANES] + both[:, LANES:]


def swap_rows(tiles, row):
    axis = tiles[0].ndim - 2
    t0, t1, t2, t3 = tiles
    up = (row & 2) == 0
    b0 = jnp.where(up, t0, pltpu.roll(t2, 2, axis))
    b2 = jnp.where(up, pltpu.roll(t0, 6, axis), t2)
    b1 = jnp.where(up, t1, pltpu.roll(t3, 2, axis))
    b3 = jnp.where(up, pltpu.roll(t1, 6, axis), t3)
    even = (row & 1) == 0
    o0 = jnp.where(even, b0, pltpu.roll(b1, 1, axis))
    o1 = jnp.where(even, pltpu.roll(b0, 7, axis), b1)
    o2 = jnp.where(even, b2, pltpu.roll(b3, 1, axis))
    o3 = jnp.where(even, pltpu.roll(b2, 7, axis), b3)
    return o0, o1, o2, o3


def swap_lanes(tiles, lane):
    axis = tiles[0].ndim - 1
    t0, t1, t2, t3 = tiles
    low = (lane & 64) == 0
    b0 = jnp.where(low, t0, pltpu.roll(t2, 64, axis))
    b2 = jnp.where(low, pltpu.roll(t0, 64, axis), t2)
    b1 = jnp.where(low, t1, pltpu.roll(t3, 64, axis))
    b3 = jnp.where(low, pltpu.roll(t1, 64, axis), t3)
    even = (lane & 32) == 0
    o0 = jnp.where(even, b0, pltpu.roll(b1, 32, axis))
    o1 = jnp.where(even, pltpu.roll(b0, 96, axis), b1)
    o2 = jnp.where(even, b2, pltpu.roll(b3, 32, axis))
    o3 = jnp.where(even, pltpu.roll(b2, 96, axis), b3)
    return o0, o1, o2, o3


def iota(shape, dim):
    return lax.broadcasted_iota(jnp.int32, shape, dim)


def transposed(tiles, row):
    axis = tiles[0].ndim - 2
    tiles = list(tiles)
    for d in (4, 2, 1):
        upper = (row & d) == 0
        for j in range(8):
            if not j & d:
                a, b = tiles[j], tiles[j + d]
                tiles[j] = jnp.where(upper, a, pltpu.roll(b, d, axis))
                tiles[j + d] = jnp.where(upper, pltpu.roll(a, 8 - d, axis), b)
    return tiles


def kernel(
    x_hbm,
    c_hbm,
    asg_hbm,
    val_hbm,
    err_hbm,
    east_hbm,
    col_hbm,
    cnt_hbm,
    o_ref,
    x_ref,
    c_ref,
    asg_ref,
    val_ref,
    err_ref,
    east_ref,
    col_ref,
    cnt_ref,
    c_next,
    rates,
    state,
    ahead,
    outgoing,
    incoming,
    returned,
    split,
    mean_of,
    maps,
    edge_out,
    edge_in,
    acc,
    part_in,
    select,
    ordered,
    x_sem,
    small_sem,
    halo_send,
    halo_recv,
    edge_send,
    edge_recv,
    part_send,
    part_recv,
    send_sem,
    early_sem,
    recv_sem,
    back_send,
    back_recv,
    everyone,
):
    g = lax.axis_index("group")
    s = lax.axis_index("slab")
    me = g * SLABS + s
    left = (me + DEVICES - 1) % DEVICES
    right = (me + 1) % DEVICES

    rate_copy = pltpu.make_async_copy(c_hbm, c_ref, small_sem.at[0])
    rate_copy.start()

    def sample_copy(quad):
        four = pl.ds(4 * quad, 4)
        return pltpu.make_async_copy(x_hbm.at[four], x_ref.at[four], x_sem.at[quad])

    for quad in range(QUADS):
        sample_copy(quad).start()
    small_copies = [
        pltpu.make_async_copy(source, target, small_sem.at[1 + i])
        for i, (source, target) in enumerate(
            [
                (asg_hbm, asg_ref),
                (val_hbm, val_ref),
                (err_hbm, err_ref),
                (east_hbm, east_ref),
                (col_hbm, col_ref),
                (cnt_hbm, cnt_ref),
            ]
        )
    ]
    for copy in small_copies:
        copy.start()

    barrier = pltpu.get_barrier_semaphore()

    def group_peer(i):
        return ((g + i) & (GROUPS - 1)) * SLABS + s

    def slab_peer(i):
        return g * SLABS + ((s + i) & (SLABS - 1))

    for i in range(1, SLABS):
        pl.semaphore_signal(
            barrier, inc=1, device_id=slab_peer(i), device_id_type=LOGICAL
        )
    for i in range(1, GROUPS):
        pl.semaphore_signal(
            barrier, inc=1, device_id=group_peer(i), device_id_type=LOGICAL
        )

    row = iota((8, LANES), 0)
    lane = iota((8, LANES), 1)
    upper_half = row < 4
    low_half = lane < 64
    z_first = (lane & (NZ - 1)) == 0

    def lanes_swapped(a, b):
        first = jnp.where(low_half, a, pltpu.roll(b, 64, 1))
        second = jnp.where(low_half, pltpu.roll(a, 64, 1), b)
        return jnp.stack([first, second])

    rate_copy.wait()

    def take_rates(source, planes, offset):
        def one(u, carry):
            for i in range(3):
                sides = [
                    lanes_swapped(source[i, u + 16 * h], source[i, u + 16 * h + 8])
                    for h in range(2)
                ]
                for x in range(planes):
                    rates[i, offset + x, pl.ds(2 * u, 2)] = jnp.where(
                        upper_half, sides[0][:, x : x + 1], sides[1][:, x : x + 1]
                    )
            return carry

        lax.fori_loop(0, 8, one, 0)

    take_rates(c_ref, PLANES, 0)

    def wrap(grid, level, first, end):
        last = grid[level, first + 1 : end + 1, 16]
        turned = pltpu.roll(last, 64, 2)
        grid[level, first + 1 : end + 1, 0] = jnp.where(
            low_half, pltpu.roll(turned, 4, 1), turned
        )

    def take_samples(quad, grid):
        sample_copy(quad).wait()

        def one(u, carry):
            tiles = []
            for h in range(2):
                for i in range(4):
                    at = 4 * quad + i
                    tiles.append(lanes_swapped(x_ref[at, u + 16 * h], x_ref[at, u + 16 * h + 8]))
            for x, tile in enumerate(transposed(tiles, row)):
                grid[0, x + 1, pl.ds(2 * u + 1, 2)] = tile
            return carry

        lax.fori_loop(0, 8, one, 0)
        wrap(grid, 0, 0, PLANES)

    def stepped(grid, level, first, end, ty, n):
        u = grid[level, first + 1 : end + 1, pl.ds(ty + 1, n)]
        above = grid[level, first:end, pl.ds(ty + 1, n)]
        below_y = grid[level, first + 1 : end + 1, pl.ds(ty, n)]
        below_z = jnp.where(z_first, pltpu.roll(u, 65, 3), pltpu.roll(u, 1, 3))
        return (
            u
            - rates[0, first:end, pl.ds(ty, n)] * (u - above)
            - rates[1, first:end, pl.ds(ty, n)] * (u - below_y)
            - rates[2, first:end, pl.ds(ty, n)] * (u - below_z)
        )

    def advance(grid, level, first, end):
        planes = end - first
        n = 16 if planes < 4 else 8

        def one(i, carry):
            new = stepped(grid, level, first, end, n * i, n)
            grid[level + 1, first + 1 : end + 1, pl.ds(n * i + 1, n)] = new
            return carry

        lax.fori_loop(0, 16 // n, one, 0)
        wrap(grid, level + 1, first, end)

    next_slab = g * SLABS + ((s + 1) & (SLABS - 1))
    last_slab = g * SLABS + ((s + SLABS - 1) & (SLABS - 1))

    def halo_copy(quad, low, high, sem):
        levels = pl.ds(low, high - low)
        return pltpu.make_async_remote_copy(
            src_ref=state.at[quad, levels, PLANES, pl.ds(1, 16)],
            dst_ref=state.at[quad, levels, 0, pl.ds(1, 16)],
            send_sem=halo_send.at[sem],
            recv_sem=halo_recv.at[sem],
            device_id=next_slab,
            device_id_type=LOGICAL,
        )

    halo_0a = halo_copy(0, 0, 3, 0)
    halo_0b = halo_copy(0, 3, STEPS, 6)
    halo_1a = halo_copy(1, 0, 3, 1)
    halo_1b = halo_copy(1, 3, STEPS, 2)

    back_halo = pltpu.make_async_remote_copy(
        src_ref=ahead.at[0, pl.ds(1, STEPS), pl.ds(1, 16)],
        dst_ref=ahead.at[0, pl.ds(PLANES + 1, STEPS), pl.ds(1, 16)],
        send_sem=halo_send.at[3],
        recv_sem=halo_recv.at[3],
        device_id=last_slab,
        device_id_type=LOGICAL,
    )
    half = pl.ds((g & 1) * (TILES // 2), TILES // 2)
    back_rates = pltpu.make_async_remote_copy(
        src_ref=c_ref.at[:, half],
        dst_ref=c_next.at[:, half],
        send_sem=halo_send.at[4],
        recv_sem=halo_recv.at[4],
        device_id=last_slab,
        device_id_type=LOGICAL,
    )
    share_rates = pltpu.make_async_remote_copy(
        src_ref=c_next.at[:, half],
        dst_ref=c_next.at[:, half],
        send_sem=halo_send.at[5],
        recv_sem=halo_recv.at[5],
        device_id=(g ^ 1) * SLABS + s,
        device_id_type=LOGICAL,
    )

    grids = [state.at[0], state.at[1]]

    def own_cone(quad):
        take_samples(quad, grids[quad])
        for level in range(STEPS - 1):
            advance(grids[quad], level, level + 3, PLANES)

    take_samples(0, grids[0])
    for level in range(2):
        advance(grids[0], level, level + 3, PLANES)
    pl.semaphore_wait(barrier, SLABS + GROUPS - 2)
    halo_0a.start()
    back_rates.start()
    for level in range(2, STEPS - 1):
        advance(grids[0], level, level + 3, PLANES)
    halo_0b.start()
    for i in range(1, GROUPS):
        pl.semaphore_signal(everyone, inc=1, device_id=group_peer(i), device_id_type=LOGICAL)
    take_samples(2, ahead)
    back_halo.start()
    own_cone(1)
    halo_1a.start()
    for level in range(STEPS - 1):
        advance(ahead, level, level + 1, PLANES)
    back_rates.wait_recv()
    share_rates.start()

    for copy in small_copies:
        copy.wait()

    slots = iota((1, OBS), 1)
    for b in range(BLOCKS):
        live = slots < cnt_ref[:, b : b + 1]
        square = jnp.where(live, 1.0 / (err_ref[b : b + 1, :] * (MEMBERS - 1.0)), 0.0)
        valued = square * val_ref[b : b + 1, :]
        easting = east_ref[b : b + 1, :]
        column = TILE_WIDTH * b - HC + col_ref[b : b + 1, :]
        at_slab = iota((SLABS, OBS), 0) == (easting >> 3)
        left_side = jnp.concatenate(
            [jnp.where(at_slab, square, 0.0), jnp.where(at_slab, valued, 0.0)], axis=0
        )
        high, low = halves(left_side)
        both = jnp.concatenate([high, low], axis=0)
        cell = iota((CELLS, OBS), 0)
        base = (easting & (PLANES - 1)) * OWN

        def spread(inside, offset):
            at = jnp.where(inside, base + column + offset, -1)
            hot = jnp.where(cell == at, 1.0, 0.0).astype(jnp.bfloat16)
            got = nt(both, hot)
            return got[: 2 * SLABS] + got[2 * SLABS :]

        maps[b] = spread((column >= 0) & (column < OWN), 0)
        if b == 0:
            edge_out[0] = spread(column < 0, OWN)
        if b == BLOCKS - 1:
            edge_out[1] = spread(column >= OWN, -OWN)

    def edge_copy(side):
        return pltpu.make_async_remote_copy(
            src_ref=edge_out.at[side],
            dst_ref=edge_in.at[side],
            send_sem=edge_send.at[side],
            recv_sem=edge_recv.at[side],
            device_id=(left, right)[side],
            device_id_type=LOGICAL,
        )

    pl.semaphore_wait(everyone, GROUPS - 1)
    edge_copy(0).start()
    edge_copy(1).start()

    spot = iota((LANES, LANES), 0)
    across = iota((LANES, LANES), 1)

    def member(r):
        return 24 * (r // 24) + 12 * ((r // 4) % 2) + 4 * (2 * ((r // 8) % 3) % 3) + r % 4

    one = jnp.float32(1.0)
    zero = jnp.float32(0.0)
    slot_lane = iota((LANES, MEMBERS), 1)
    slot_spot = iota((LANES, MEMBERS), 0)
    hot = jnp.where(asg_ref[...] == slot_spot, one, zero).astype(jnp.bfloat16)
    order = jnp.where((member(spot) == across) & (spot < MEMBERS), one, zero).astype(jnp.bfloat16)
    slot_order = jnp.where((member(slot_spot) == slot_lane) & (slot_spot < MEMBERS), one, zero)
    member_rows = nn(order, hot).astype(jnp.bfloat16)
    select[...] = nt(member_rows, slot_order.astype(jnp.bfloat16)).astype(jnp.bfloat16)

    early = pl.ds(0, 2)

    def send_early():
        def send(k, carry):
            peer = (((g + (k >> 4)) & (GROUPS - 1)) * SLABS) + ((s + k) & (SLABS - 1))
            pltpu.make_async_remote_copy(
                src_ref=outgoing.at[peer, early],
                dst_ref=incoming.at[s * GROUPS + g, early],
                send_sem=send_sem.at[0],
                recv_sem=early_sem,
                device_id=peer,
                device_id_type=LOGICAL,
            ).start()
            return carry

        lax.fori_loop(1, DEVICES, send, 0, unroll=2)

    def slab_of(i, c, sign):
        z = (s >> 2) + sign * (c + i)
        y = s + sign * c
        return ((z & 3) << 2) | (y & 3)

    def send_last(k, carry):
        peer_g = (g + (k >> 2) + 2 * k) & (GROUPS - 1)
        peer_s = slab_of(k >> 5, k & 3, 1)
        peer = peer_g * SLABS + peer_s
        pltpu.make_async_remote_copy(
            src_ref=outgoing.at[peer, 2],
            dst_ref=incoming.at[s * GROUPS + g, 2],
            send_sem=send_sem.at[1],
            recv_sem=recv_sem.at[s],
            device_id=peer,
            device_id_type=LOGICAL,
        ).start()
        return carry

    def pack_all(slot, grid, first):
        def pack(i, carry):
            ty = 4 * i
            new = stepped(grid, STEPS - 1, first, first + PLANES, ty, 4)
            at_plane = [new[(x - first) % PLANES] for x in range(PLANES)]
            for h in range(2):
                tiles = []
                for x in range(4):
                    a, b = at_plane[x], at_plane[4 + x]
                    if h == 0:
                        tiles.append(jnp.where(upper_half, a, pltpu.roll(b, 4, 1)))
                    else:
                        tiles.append(jnp.where(upper_half, pltpu.roll(a, 4, 1), b))
                for j, tile in enumerate(swap_lanes(tiles, lane)):
                    for k in range(4):
                        at = 64 * h + 32 * (j // 2) + 2 * k + j % 2
                        outgoing[at + 2 * ty, slot] = tile[k]
            return carry

        lax.fori_loop(0, 4, pack, 0)

    halo_0b.wait_send()
    halo_1b.start()
    halo_0a.wait_recv()
    for level in range(3):
        advance(grids[0], level, 0, level + 3)
    halo_0b.wait_recv()
    for level in range(3, STEPS - 1):
        advance(grids[0], level, 0, level + 3)
    pack_all(0, grids[0], 0)
    share_rates.wait_recv()
    take_rates(c_next, STEPS, PLANES)
    back_halo.wait_recv()
    wrap(ahead, 0, PLANES, PLANES + STEPS)
    for level in range(STEPS - 1):
        advance(ahead, level, PLANES, PLANES + STEPS)
    pack_all(1, ahead, STEPS)
    send_early()
    halo_1a.wait_recv()
    for level in range(3):
        advance(grids[1], level, 0, level + 3)
    halo_1b.wait_recv()
    for level in range(3, STEPS - 1):
        advance(grids[1], level, 0, level + 3)
    pack_all(2, grids[1], 0)
    lax.fori_loop(1, DEVICES, send_last, 0, unroll=2)
    incoming[s * GROUPS + g] = outgoing[me]

    edge_copy(0).wait_recv()
    edge_copy(1).wait_recv()
    maps[BLOCKS] = edge_in[1]
    maps[BLOCKS + 1] = edge_in[0]
    acc[...] = jnp.zeros(acc.shape, jnp.float32)

    half_row = iota((12, 8, LANES), 1) < 4
    pad = jnp.zeros((LANES - MEMBERS, CELLS), jnp.bfloat16)

    late = (iota((GROUPS, 8, LANES), 1) >= 4) & (iota((GROUPS, 8, LANES), 2) >= 64)
    most = incoming.at[pl.ds(0, DEVICES - 1), early]
    pltpu.make_async_copy(most, most, early_sem).wait()
    seven = incoming.at[pl.ds(0, GROUPS - 1), 2]
    pltpu.make_async_copy(seven, seven, recv_sem.at[s]).wait()

    def gather(i, carry):
        slabs = [slab_of(i >> 1, 2 * (i & 1) + k, -1) for k in range(2)]
        eight = incoming.at[pl.ds(0, GROUPS), 2]

        @pl.when(i > 0)
        def _():
            pltpu.make_async_copy(eight, eight, recv_sem.at[slabs[0]]).wait()

        pltpu.make_async_copy(eight, eight, recv_sem.at[slabs[1]]).wait()
        highs, lows, sides = [], [], []
        for k in range(2):
            from_slab = slabs[k]
            before = (from_slab - 1) & (SLABS - 1)
            got = incoming[pl.ds(GROUPS * from_slab, GROUPS)]
            ahead_of = jnp.where(late, got[:, 1], incoming[pl.ds(GROUPS * before, GROUPS), 1])
            got = jnp.concatenate([got[:, :1], ahead_of[:, None], got[:, 2:]], axis=1)
            got = got.reshape(4, 2, QUADS, 8, LANES)
            a = got[:, 0].reshape(12, 8, LANES)
            b = got[:, 1].reshape(12, 8, LANES)
            near = jnp.where(half_row, a, pltpu.roll(b, 4, 1)).reshape(MEMBERS, LANES)
            far = jnp.where(half_row, pltpu.roll(a, 4, 1), b).reshape(MEMBERS, LANES)
            field = jnp.concatenate([near, far], axis=1)
            mean = jnp.sum(field, axis=0, keepdims=True) * (1.0 / MEMBERS)
            mean_of[from_slab] = mean
            away = field - mean
            high, low = halves(away)
            right_side = jnp.concatenate([high, pad, low, pad], axis=0)
            split[from_slab] = right_side
            pieces = []
            for b in range(BLOCKS + 2):
                omega = maps[b, pl.ds(from_slab, 1)]
                v = maps[b, pl.ds(SLABS + from_slab, 1)]
                pieces.append(omega * away)
                pieces.append(jnp.broadcast_to(v - mean * omega, (ROWS - MEMBERS, CELLS)))
            lhs_high, lhs_low = halves(jnp.concatenate(pieces, axis=0))
            highs.append(lhs_high)
            lows.append(lhs_low)
            sides.append(right_side)
        side = jnp.concatenate(sides, axis=1)
        high_part = nt(jnp.concatenate(highs, axis=1), side)
        low_part = nt(jnp.concatenate(lows, axis=1), side[:LANES])
        total = high_part[:, :LANES] + high_part[:, LANES:] + low_part
        acc[...] += total.reshape(acc.shape)
        return carry

    lax.fori_loop(0, SLABS // 2, gather, 0)

    def part_copy(side):
        return pltpu.make_async_remote_copy(
            src_ref=acc.at[BLOCKS + side],
            dst_ref=part_in.at[side],
            send_sem=part_send.at[side],
            recv_sem=part_recv.at[side],
            device_id=(left, right)[side],
            device_id_type=LOGICAL,
        )

    part_copy(0).start()
    part_copy(1).start()

    identity = jnp.where((spot == across) & (spot < MEMBERS), one, zero)[:MEMBERS]
    part_copy(0).wait_recv()
    part_copy(1).wait_recv()
    totals = [acc[b] for b in range(BLOCKS)]
    totals[BLOCKS - 1] = totals[BLOCKS - 1] + part_in[0]
    totals[0] = totals[0] + part_in[1]
    grams = [identity + t[:MEMBERS] for t in totals]
    fros = [jnp.sqrt(jnp.sum(t * t, keepdims=True)) for t in grams]
    a_of = [t / f for t, f in zip(grams, fros)]
    middles = [1.5 * identity - 0.5 * a for a in a_of]
    z_of = middles
    a_of = [product(a, r) for a, r in zip(a_of, middles)]
    for iteration in range(1, ITERS):
        middles = [1.5 * identity - 0.5 * product(z, a) for z, a in zip(z_of, a_of)]
        if iteration < ITERS - 1:
            a_of = [product(a, r) for a, r in zip(a_of, middles)]
        z_of = [product(r, z) for r, z in zip(middles, z_of)]
    for b in range(BLOCKS):
        transform = z_of[b] * (1.0 / jnp.sqrt(fros[b]))
        projected = jnp.broadcast_to(totals[b][MEMBERS : MEMBERS + 1], (16, LANES))
        mean_weights = product(product(projected, transform), transform)[:1]
        high, low = halves(transform)
        both = nn(select[...], jnp.concatenate([padded(high), padded(low)], axis=1))
        by_member = (both[:MEMBERS, :LANES] + both[:MEMBERS, LANES:]) + mean_weights
        high, low = halves(by_member)
        ordered[0, MEMBERS * b : MEMBERS * (b + 1)] = jnp.concatenate([high, high], axis=1)
        ordered[1, MEMBERS * b : MEMBERS * (b + 1)] = jnp.concatenate([low, low], axis=1)

    for i, part in enumerate((early, 2)):
        most = outgoing.at[pl.ds(0, DEVICES - 1), part]
        pltpu.make_async_copy(most, most, send_sem.at[i]).wait()

    block_of = (iota((MEMBERS, CELLS), 1) % OWN) // TILE_WIDTH

    def give_back(i, carry):
        to_slabs = []
        for c in range(4):
            to_slab = slab_of(i, c, 1)
            to_slabs.append(to_slab)
            right_side = split[to_slab]
            parts = nn(ordered[0], right_side) + nn(ordered[1], right_side)
            field = parts[:MEMBERS]
            for b in range(1, BLOCKS):
                field = jnp.where(block_of == b, parts[MEMBERS * b : MEMBERS * (b + 1)], field)
            field = field + mean_of[to_slab]
            near = field[:, :LANES].reshape(12, 8, LANES)
            far = field[:, LANES:].reshape(12, 8, LANES)
            even = jnp.where(half_row, near, pltpu.roll(far, 4, 1)).reshape(4, QUADS, 8, LANES)
            odd = jnp.where(half_row, pltpu.roll(near, 4, 1), far).reshape(4, QUADS, 8, LANES)
            for a in range(4):
                incoming[GROUPS * to_slab + 2 * a] = even[a]
                incoming[GROUPS * to_slab + 2 * a + 1] = odd[a]

        def to_group(j, carry):
            for c in range(4):
                peer_g = (g + j + 2 * c) & (GROUPS - 1)

                def start():
                    pltpu.make_async_remote_copy(
                        src_ref=incoming.at[GROUPS * to_slabs[c] + peer_g],
                        dst_ref=returned.at[me],
                        send_sem=back_send,
                        recv_sem=back_recv,
                        device_id=peer_g * SLABS + to_slabs[c],
                        device_id_type=LOGICAL,
                    ).start()

                if c == 0:
                    pl.when(i * GROUPS + j > 0)(start)
                else:
                    start()
            return carry

        lax.fori_loop(0, GROUPS, to_group, 0)
        return carry

    lax.fori_loop(0, 4, give_back, 0)
    returned[me] = incoming[s * GROUPS + g]

    for copy in (halo_0a, halo_1a, halo_1b, back_halo, back_rates, share_rates):
        copy.wait_send()
    for side in range(2):
        edge_copy(side).wait_send()
        part_copy(side).wait_send()
    sent = incoming.at[pl.ds(0, DEVICES - 1)]
    pltpu.make_async_copy(sent, sent, back_send).wait()
    got = returned.at[pl.ds(0, DEVICES - 1)]
    pltpu.make_async_copy(got, got, back_recv).wait()

    def unpack(tile, carry):
        for quad in range(QUADS):
            tiles = swap_lanes([returned[4 * tile + q, quad] for q in range(4)], lane)
            tiles = swap_rows(tiles, row)
            for i in range(4):
                o_ref[4 * (2 * quad % 3) + i, tile] = tiles[i]
        return carry

    lax.fori_loop(0, TILES, unpack, 0, unroll=4)


def shards(
    initial_samples,
    transport_ratios,
    assignment,
    obs_values,
    obs_error,
    sensor_easting_offset,
    obs_column,
    obs_count,
):
    members, planes, columns = initial_samples.shape

    def tiled(x):
        return jnp.transpose(x.reshape(-1, planes, TILES, LANES), (0, 2, 1, 3))

    f32 = jnp.float32
    i32 = jnp.int32
    bf16 = jnp.bfloat16
    dma = pltpu.SemaphoreType.DMA
    hbm = pl.BlockSpec(memory_space=pltpu.HBM)
    out = pl.pallas_call(
        kernel,
        name="analysis",
        out_shape=jax.ShapeDtypeStruct((members, TILES, planes, LANES), f32),
        in_specs=[hbm] * 8,
        out_specs=pl.BlockSpec(memory_space=pltpu.VMEM),
        scratch_shapes=[
            pltpu.VMEM((4 * QUADS, TILES, PLANES, LANES), f32),
            pltpu.VMEM((3, TILES, PLANES, LANES), f32),
            pltpu.VMEM((1, MEMBERS), i32),
            pltpu.VMEM((BLOCKS, OBS), f32),
            pltpu.VMEM((BLOCKS, OBS), f32),
            pltpu.VMEM((BLOCKS, OBS), i32),
            pltpu.VMEM((BLOCKS, OBS), i32),
            pltpu.VMEM((1, BLOCKS), i32),
            pltpu.VMEM((3, TILES, PLANES, LANES), f32),
            pltpu.VMEM((3, PLANES + STEPS, 16, 8, LANES), f32),
            pltpu.VMEM((2, STEPS, PLANES + 1, 17, 8, LANES), f32),
            pltpu.VMEM((STEPS, PLANES + STEPS + 1, 17, 8, LANES), f32),
            pltpu.VMEM((DEVICES, QUADS, 8, LANES), f32),
            pltpu.VMEM((DEVICES, QUADS, 8, LANES), f32),
            pltpu.VMEM((DEVICES, QUADS, 8, LANES), f32),
            pltpu.VMEM((SLABS, 2 * LANES, CELLS), bf16),
            pltpu.VMEM((SLABS, 1, CELLS), f32),
            pltpu.VMEM((BLOCKS + 2, 2 * SLABS, CELLS), f32),
            pltpu.VMEM((2, 2 * SLABS, CELLS), f32),
            pltpu.VMEM((2, 2 * SLABS, CELLS), f32),
            pltpu.VMEM((BLOCKS + 2, ROWS, LANES), f32),
            pltpu.VMEM((2, ROWS, LANES), f32),
            pltpu.VMEM((LANES, LANES), bf16),
            pltpu.VMEM((2, BLOCKS * MEMBERS, 2 * LANES), bf16),
            dma((QUADS,)),
            dma((7,)),
            dma((7,)),
            dma((7,)),
            dma((2,)),
            dma((2,)),
            dma((2,)),
            dma((2,)),
            dma((2,)),
            dma,
            dma((SLABS,)),
            dma,
            dma,
            pltpu.SemaphoreType.REGULAR,
        ],
        compiler_params=pltpu.CompilerParams(
            collective_id=0, has_side_effects=True, vmem_limit_bytes=56 << 20
        ),
    )(
        tiled(initial_samples),
        tiled(transport_ratios),
        assignment[None, :],
        obs_values,
        obs_error,
        sensor_easting_offset,
        obs_column,
        obs_count[None, :],
    )
    return jnp.transpose(out, (0, 2, 1, 3)).reshape(members, planes, columns)


def solution(mesh):
    placed = (
        P("group", "slab", None),
        P(None, "slab", None),
        P(),
        P(("group", "slab"), None),
        P(("group", "slab"), None),
        P(("group", "slab"), None),
        P(("group", "slab"), None),
        P(("group", "slab")),
    )
    return jax.shard_map(
        shards, mesh=mesh, in_specs=placed, out_specs=P("group", "slab", None), check_vma=False
    )
```
